128 devices in a mesh: row: 32 (over y, z_lo, x), col: 4 (over z_hi, core).
Axes of the slice: x: 4, y: 4, z: 4 (z_hi: 2, z_lo: 2; z = z_hi * 2 + z_lo), core: 2. Of those that a mesh axis runs over, the one named last changes fastest.
Arguments:
- samples: float32 [131072, 32], P(('row', 'col')), may hold values from -3 to 3
- sample_logw: float32 [131072], P(('row', 'col')), may hold values from -8 to 8
- references: float32 [65536, 32], P(('row', 'col')), may hold values from -3 to 3
- reference_logw: float32 [65536], P(('row', 'col')), may hold values from -8 to 8
- dual_start: float32 [32, 4096], P('row'), may hold values from -3 to 3
- kept_tiles: int32 [32, 4, 32], P('row', 'col'), may hold values from 0 to 255, as said below
- tile_counts: int32 [32, 4], P('row', 'col'), may hold values from 2 to 32, as said below
Outputs:
- row_duals: float32 [32, 4096], P('row')
- col_duals: float32 [4, 16384], P('col')
The draws below stay inside these ranges and needn't reach their ends.
Inputs may be any that keep to these rules, and one draw needn't show every extreme that they name: `kept_tiles`: on device (i, j) the first tile_counts[i, j] entries are distinct tiles r * 32 + c of its 8 by 32 grid; later entries are tiles of that grid and unused. Every block of every sample group and of every reference group lies in some used tile. `tile_counts`: 32 on at least one device.
All inputs are finite; a program needn't handle non-finite values.
Results may differ from the reference program's by a relative error of at most 0.0003.
Values sent between devices are 32-bit elements; how exact they have to be, the bound alone decides.
A program may use at most 64 MiB of HBM per device.

```python
import jax
import jax.numpy as jnp
from jax import lax

TILE = 512
DIM = 32
ITERS = 3
KSLOT = 32
RBD = 8
CBD = 32
SAMPLES = 131072
POINTS = 65536
N_ROW = 32
N_COL = 4


def guaranteed():
    return max((RBD + N_COL - 1) // N_COL, (CBD + N_ROW - 1) // N_ROW)


def draw_kept_tiles(key, part):
    count_guard = guaranteed()
    cells = RBD * CBD

    def single(index):
        row_index = index // N_COL
        col_index = index % N_COL
        places = jnp.arange(count_guard, dtype=jnp.int32)
        rows = (col_index + N_COL * places) % RBD
        cols = (row_index + N_ROW * places) % CBD
        chosen = rows * CBD + cols
        scores = jax.random.permutation(jax.random.fold_in(jax.random.fold_in(key, 7), index), cells).astype(jnp.int32) + count_guard
        scores = scores.at[chosen].set(places)
        order = jnp.argsort(scores, stable=True)
        return order[:KSLOT].astype(jnp.int32)
    tiles = jax.vmap(single)(jnp.arange(N_ROW * N_COL, dtype=jnp.int32))
    return tiles.reshape(N_ROW, N_COL, KSLOT)


def draw_tile_counts(key, part):
    bottom = guaranteed()
    pairs = N_ROW // 2 * N_COL
    heavy = jax.random.randint(jax.random.fold_in(key, 11), (pairs,), bottom, KSLOT + 1, dtype=jnp.int32)
    busiest = jax.random.randint(jax.random.fold_in(key, 13), (), 0, pairs, dtype=jnp.int32)
    heavy = heavy.at[busiest].set(KSLOT)
    light_top = KSLOT + bottom - heavy + 1
    light = jax.random.randint(jax.random.fold_in(key, 19), (pairs,), bottom, light_top, dtype=jnp.int32)
    light = light.at[busiest].set(bottom)
    flips = jax.random.randint(jax.random.fold_in(key, 23), (pairs,), 0, 2, dtype=jnp.int32)
    first = jnp.where(flips == 0, heavy, light)
    second = jnp.where(flips == 0, light, heavy)
    first = first.reshape(N_ROW // 2, N_COL)
    second = second.reshape(N_ROW // 2, N_COL)
    counts = jnp.stack([first, second], axis=1).reshape(N_ROW, N_COL)
    return counts.astype(jnp.int32)


def draw_dual_start(key, part):
    values = jnp.clip(jax.random.normal(jax.random.fold_in(key, 17), (N_ROW, RBD * TILE), jnp.float32), -3.0, 3.0)
    return values


def block_levels(key, shape, shards, least, top_value):
    gain = 1.0
    for dim, parts in shards:
        heights = jax.random.uniform(jax.random.fold_in(jax.random.fold_in(key, 6), dim), (parts,), jnp.float32, least / len(shards), top_value / len(shards))
        gain = gain * jnp.repeat(jnp.exp(heights), shape[dim] // parts).reshape((-1,) + (1,) * (len(shape) - 1 - dim))
    return gain


def centred(stream_key, extent, spread, limit, cuts=(), held_as=jnp.bfloat16):
    values = spread * jax.random.normal(stream_key, extent, jnp.float32)
    if cuts:
        values = values * block_levels(stream_key, extent, cuts, -0.22, 0.18)
    return jnp.clip(values, -limit, limit).astype(held_as)


def setup_inputs(seed: int = 0) -> dict:
    splits = jax.random.split(jax.random.key(seed), 8)
    return {
        "samples": centred(splits[0], (SAMPLES, DIM), 0.5, 3.0, ((0, 128),), jnp.float32),
        "sample_logw": centred(splits[1], (SAMPLES,), 2.0, 8.0, ((0, 128),), jnp.float32),
        "references": centred(splits[2], (POINTS, DIM), 0.5, 3.0, ((0, 128),), jnp.float32),
        "reference_logw": centred(splits[3], (POINTS,), 2.0, 8.0, ((0, 128),), jnp.float32),
        "dual_start": draw_dual_start(jax.random.fold_in(splits[7], 71), 0),
        "kept_tiles": draw_kept_tiles(jax.random.fold_in(splits[7], 71), 0),
        "tile_counts": draw_tile_counts(jax.random.fold_in(splits[7], 71), 0),
    }


lowest = -1.0e30
epsilon = 0.1


def combine(left, right):
    peak = jnp.maximum(left[0], right[0])
    return (peak, left[1] * jnp.exp(left[0] - peak) + right[1] * jnp.exp(right[0] - peak))


def tile_cost(row_points, col_points):
    inner = jnp.dot(row_points, col_points.T, precision=lax.Precision.HIGHEST, preferred_element_type=jnp.float32)
    row_norms = jnp.sum(row_points * row_points, axis=1)
    col_norms = jnp.sum(col_points * col_points, axis=1)
    return row_norms[:, None] + col_norms[None, :] - 2.0 * inner


def partials(x_group, x_weights, y_group, y_weights, duals, tiles, count, by_column):
    width = y_group.shape[0] if by_column else x_group.shape[0]
    col_blocks = y_group.shape[0] // TILE

    def visit(carry, slot):
        tile = tiles[slot]
        row_start = ((tile // col_blocks) * TILE).astype(jnp.int32)
        col_start = ((tile % col_blocks) * TILE).astype(jnp.int32)
        row_points = lax.dynamic_slice_in_dim(x_group, row_start, TILE, 0)
        col_points = lax.dynamic_slice_in_dim(y_group, col_start, TILE, 0)
        cost = tile_cost(row_points, col_points)
        if by_column:
            weights = lax.dynamic_slice_in_dim(x_weights, row_start, TILE, 0)
            dual_part = lax.dynamic_slice_in_dim(duals, row_start, TILE, 0)
            score = weights[:, None] + (dual_part[:, None] - cost) / epsilon
            peak = jnp.max(score, axis=0)
            total = jnp.sum(jnp.exp(score - peak[None, :]), axis=0)
            start = col_start
        else:
            weights = lax.dynamic_slice_in_dim(y_weights, col_start, TILE, 0)
            dual_part = lax.dynamic_slice_in_dim(duals, col_start, TILE, 0)
            score = weights[None, :] + (dual_part[None, :] - cost) / epsilon
            peak = jnp.max(score, axis=1)
            total = jnp.sum(jnp.exp(score - peak[:, None]), axis=1)
            start = row_start
        valid = slot < count
        peak = jnp.where(valid, peak, lowest)
        total = jnp.where(valid, total, 0.0)
        before = (lax.dynamic_slice_in_dim(carry[0], start, TILE, 0), lax.dynamic_slice_in_dim(carry[1], start, TILE, 0))
        merged = combine(before, (peak, total))
        return (lax.dynamic_update_slice_in_dim(carry[0], merged[0], start, 0), lax.dynamic_update_slice_in_dim(carry[1], merged[1], start, 0)), None

    start_state = (jnp.full((width,), lowest, jnp.float32), jnp.zeros((width,), jnp.float32))
    result, unused = lax.scan(visit, start_state, jnp.arange(tiles.shape[0], dtype=jnp.int32))
    return result


def reference(samples, sample_logw, references, reference_logw, dual_start, kept_tiles, tile_counts):
    row_width = RBD * TILE
    col_width = CBD * TILE
    x_groups = samples.reshape(N_ROW, row_width, DIM)
    x_weights = sample_logw.reshape(N_ROW, row_width)
    y_groups = references.reshape(N_ROW, N_COL, col_width // N_ROW, DIM).transpose(1, 0, 2, 3).reshape(N_COL, col_width, DIM)
    y_weights = reference_logw.reshape(N_ROW, N_COL, col_width // N_ROW).transpose(1, 0, 2).reshape(N_COL, col_width)
    devices = jnp.arange(N_ROW * N_COL, dtype=jnp.int32)

    def column_pass(row_duals):
        def single(index):
            row_index = index // N_COL
            col_index = index % N_COL
            return partials(x_groups[row_index], x_weights[row_index], y_groups[col_index], y_weights[col_index], row_duals[row_index], kept_tiles[row_index, col_index], tile_counts[row_index, col_index], True)

        peaks, totals = lax.map(single, devices)
        peaks = peaks.reshape(N_ROW, N_COL, col_width)
        totals = totals.reshape(N_ROW, N_COL, col_width)
        peak = jnp.max(peaks, axis=0)
        total = jnp.sum(totals * jnp.exp(peaks - peak[None]), axis=0)
        return -epsilon * (peak + jnp.log(total))

    def row_pass(col_duals):
        def single(index):
            row_index = index // N_COL
            col_index = index % N_COL
            return partials(x_groups[row_index], x_weights[row_index], y_groups[col_index], y_weights[col_index], col_duals[col_index], kept_tiles[row_index, col_index], tile_counts[row_index, col_index], False)

        peaks, totals = lax.map(single, devices)
        peaks = peaks.reshape(N_ROW, N_COL, row_width)
        totals = totals.reshape(N_ROW, N_COL, row_width)
        peak = jnp.max(peaks, axis=1)
        total = jnp.sum(totals * jnp.exp(peaks - peak[:, None]), axis=1)
        return -epsilon * (peak + jnp.log(total))

    row_duals = dual_start
    col_duals = jnp.zeros((N_COL, col_width), jnp.float32)
    for turn in range(ITERS):
        col_duals = column_pass(row_duals)
        row_duals = row_pass(col_duals)
    return row_duals, col_duals
```

```python
import functools

import jax
import jax.numpy as jnp
from jax import lax
from jax.experimental import pallas as pl
from jax.experimental.pallas import tpu as pltpu
from jax.sharding import PartitionSpec as P

TILE = 512
ITERS = 3
LANES = 128
PIECES = TILE // LANES
DEPTH = 128
BIAS = 16
MESH = pl.DeviceIdType.MESH

lowest = -1e30
epsilon = 0.1
LOG2E = 1.4426950408889634
LN2 = 0.6931471805599453
SCALE = 2.0 / epsilon * LOG2E


def lse(values):
    peak = jnp.max(values, axis=0, keepdims=True)
    return peak + jnp.log2(jnp.sum(jnp.exp2(values - peak), axis=0, keepdims=True))


def halves(values):
    high = values.astype(jnp.bfloat16)
    low = (values - high.astype(jnp.float32)).astype(jnp.bfloat16)
    return high, low


def place_points(points, reduced, kept, slot):
    high, low = halves(points)
    dim = points.shape[0]
    top = BIAS + 3 * dim
    for ref, order in ((reduced, (high, high, low)), (kept, (high, low, high))):
        for k, part in enumerate(order):
            ref[slot, BIAS + k * dim : BIAS + (k + 1) * dim, :] = part
        ref[slot, top:, :] = jnp.zeros((DEPTH - top, TILE), jnp.bfloat16)
    kept[slot, :BIAS, :] = jnp.ones((BIAS, TILE), jnp.bfloat16)


def place_bias(rows, reduced, slot):
    index = lax.broadcasted_iota(jnp.int32, (BIAS, LANES), 0)
    for piece in range(PIECES):
        row = rows[piece : piece + 1, :]
        first = row.astype(jnp.bfloat16).astype(jnp.float32)
        rest = row - first
        second = rest.astype(jnp.bfloat16).astype(jnp.float32)
        third = rest - second
        tile = jnp.where(
            index == 0,
            first,
            jnp.where(index == 1, second, jnp.where(index == 2, third, 0.0)),
        )
        reduced[slot, :BIAS, piece * LANES : (piece + 1) * LANES] = tile.astype(jnp.bfloat16)


def cut(line):
    return [line[:, k * LANES : (k + 1) * LANES] for k in range(PIECES)]


def kernel(
    n_row,
    n_col,
    tiles,
    col_ids,
    row_ids,
    x_own,
    xw_own,
    y_own,
    yw_own,
    start,
    row_out,
    col_out,
    x_all,
    xw_all,
    y_all,
    x_reduced,
    x_kept,
    y_reduced,
    y_kept,
    x_norm,
    score_a,
    score_b,
    peak_a,
    peak_b,
    slots,
    col_part,
    col_recv,
    col_send,
    bias_all,
    row_part,
    row_recv,
    row_total,
    x_ssem,
    x_rsem,
    w_ssem,
    w_rsem,
    y_ssem,
    y_rsem,
    c_ssem,
    c_rsem,
    b_ssem,
    b_rsem,
    r_ssem,
    r_rsem,
):
    me_row = lax.axis_index("row")
    me_col = lax.axis_index("col")
    n_slot = slots.shape[0]
    row_blocks = x_all.shape[0]
    own_blocks = x_own.shape[0]

    def along_row(d):
        return lax.rem(me_row + d, n_row)

    def along_col(d):
        return lax.rem(me_col + d, n_col)

    barrier = pltpu.get_barrier_semaphore()

    def greet(d, carry):
        pl.semaphore_signal(
            barrier, inc=1, device_id={"row": along_row(d)}, device_id_type=MESH
        )
        return carry

    lax.fori_loop(1, n_row, greet, 0)
    for d in range(1, n_col):
        pl.semaphore_signal(
            barrier, inc=1, device_id={"col": along_col(d)}, device_id_type=MESH
        )
    pl.semaphore_wait(barrier, n_row - 1 + n_col - 1)

    def x_copy(target, owner):
        return pltpu.make_async_remote_copy(
            src_ref=x_own,
            dst_ref=x_all.at[pl.ds(owner * own_blocks, own_blocks)],
            send_sem=x_ssem.at[target],
            recv_sem=x_rsem.at[owner],
            device_id={"col": target},
            device_id_type=MESH,
        )

    def w_copy(target, owner):
        return pltpu.make_async_remote_copy(
            src_ref=xw_own,
            dst_ref=xw_all.at[pl.ds(owner * own_blocks, own_blocks)],
            send_sem=w_ssem.at[target],
            recv_sem=w_rsem.at[owner],
            device_id={"col": target},
            device_id_type=MESH,
        )

    def y_copy(target, owner):
        return pltpu.make_async_remote_copy(
            src_ref=y_own,
            dst_ref=y_all.at[owner],
            send_sem=y_ssem.at[target],
            recv_sem=y_rsem.at[owner],
            device_id={"row": target},
            device_id_type=MESH,
        )

    def c_copy(it, target, owner):
        return pltpu.make_async_remote_copy(
            src_ref=col_part.at[it, target],
            dst_ref=col_recv.at[it, owner],
            send_sem=c_ssem.at[it, target],
            recv_sem=c_rsem.at[it, owner],
            device_id={"row": target},
            device_id_type=MESH,
        )

    def b_copy(it, target, owner):
        return pltpu.make_async_remote_copy(
            src_ref=col_send.at[it],
            dst_ref=bias_all.at[it, owner],
            send_sem=b_ssem.at[it, target],
            recv_sem=b_rsem.at[it, owner],
            device_id={"row": target},
            device_id_type=MESH,
        )

    def r_copy(it, target, owner):
        return pltpu.make_async_remote_copy(
            src_ref=row_part.at[it],
            dst_ref=row_recv.at[it, owner],
            send_sem=r_ssem.at[it, target],
            recv_sem=r_rsem.at[it, owner],
            device_id={"col": target},
            device_id_type=MESH,
        )

    for d in range(1, n_col):
        x_copy(along_col(d), me_col).start()
        w_copy(along_col(d), me_col).start()

    def y_start(d, carry):
        y_copy(along_row(d), me_row).start()
        return carry

    lax.fori_loop(1, n_row, y_start, 0)

    place_points(y_own[...], y_reduced, y_kept, me_row)
    y_norm = jnp.sum(y_own[...] * y_own[...], axis=0, keepdims=True)
    for d in range(own_blocks):
        x_all[me_col * own_blocks + d] = x_own[d]
        xw_all[me_col * own_blocks + d] = xw_own[d]
    for d in range(1, n_col):
        x_copy(me_col, along_col(d)).wait_recv()
        w_copy(me_col, along_col(d)).wait_recv()

    def x_block(b, carry):
        points = x_all[b]
        place_points(points * SCALE, x_reduced, x_kept, b)
        norm = cut(jnp.sum(points * points, axis=0, keepdims=True))
        for k in range(PIECES):
            x_norm[b, k : k + 1, :] = norm[k]
        bias = xw_all[b] + (start[b] - x_norm[b]) * (1.0 / epsilon)
        place_bias(bias * LOG2E, x_reduced, b)
        return carry

    lax.fori_loop(0, row_blocks, x_block, 0)

    def y_block(d, carry):
        owner = along_row(d)
        y_copy(me_row, owner).wait_recv()
        place_points(y_all[owner], y_reduced, y_kept, owner)
        return carry

    lax.fori_loop(1, n_row, y_block, 0)

    def visit(reduced, kept, by_column):
        def begin(slot, score, peak):
            tile = tiles[lax.rem(slot, n_slot)]
            row = lax.div(tile, n_row)
            col = lax.rem(tile, n_row)
            left, right = (row, col) if by_column else (col, row)
            value = lax.dot_general(
                reduced[left],
                kept[right],
                (((0,), (0,)), ((), ())),
                preferred_element_type=jnp.float32,
            )
            score[...] = value
            peak[...] = jnp.max(value, axis=0, keepdims=True)

        def finish(slot, score, peak):
            top = peak[...]
            total = jnp.sum(jnp.exp2(score[...] - top), axis=0, keepdims=True)
            slots[pl.ds(slot, 1), :] = top + jnp.log2(total)

        begin(0, score_a, peak_a)

        def pair(i, carry):
            begin(2 * i + 1, score_b, peak_b)
            finish(2 * i, score_a, peak_a)
            begin(2 * i + 2, score_a, peak_a)
            finish(2 * i + 1, score_b, peak_b)
            return carry

        lax.fori_loop(0, n_slot // 2, pair, 0)

    def fold(ids, block):
        return cut(lse(jnp.where(ids[...] == block, slots[...], lowest)))

    def iteration(it, carry):
        visit(x_reduced, y_kept, True)

        def col_fold(c, inner):
            line = fold(col_ids, c)
            for k in range(PIECES):
                col_part[it, c, k : k + 1, :] = line[k]
            return inner

        lax.fori_loop(0, n_row, col_fold, 0)

        def c_start(d, inner):
            c_copy(it, along_row(d), me_row).start()
            return inner

        lax.fori_loop(1, n_row, c_start, 0)
        col_recv[it, me_row] = col_part[it, me_row]

        def c_wait(d, inner):
            c_copy(it, me_row, along_row(d)).wait_recv()
            return inner

        lax.fori_loop(1, n_row, c_wait, 0)
        total = lse(col_recv[it])[0]
        bias = yw_own[...] * LOG2E - total
        norm = cut(y_norm)
        for k in range(PIECES):
            col_send[it, k : k + 1, :] = bias[k : k + 1]
            dual = norm[k] - (epsilon * LN2) * total[k : k + 1]
            col_send[it, PIECES + k : PIECES + k + 1, :] = dual

        def b_start(d, inner):
            b_copy(it, along_row(d), me_row).start()
            return inner

        lax.fori_loop(1, n_row, b_start, 0)
        bias_all[it, me_row] = col_send[it]

        place_bias(bias_all[it, me_row], y_reduced, me_row)

        def b_wait(d, inner):
            owner = along_row(d)
            b_copy(it, me_row, owner).wait_recv()
            place_bias(bias_all[it, owner], y_reduced, owner)
            return inner

        lax.fori_loop(1, n_row, b_wait, 0)

        visit(y_reduced, x_kept, False)

        def row_fold(b, inner):
            line = fold(row_ids, b)
            for k in range(PIECES):
                row_part[it, b, k : k + 1, :] = line[k]
            return inner

        lax.fori_loop(0, row_blocks, row_fold, 0)
        for d in range(1, n_col):
            r_copy(it, along_col(d), me_col).start()
        row_recv[it, me_col] = row_part[it]
        for d in range(1, n_col):
            r_copy(it, me_col, along_col(d)).wait_recv()
        row_total[...] = lse(row_recv[it])[0]

        def row_bias(b, inner):
            place_bias(xw_all[b] * LOG2E - row_total[b], x_reduced, b)
            return inner

        lax.fori_loop(0, row_blocks, row_bias, 0)
        return carry

    lax.fori_loop(0, ITERS, iteration, 0)

    row_out[...] = x_norm[...] - (epsilon * LN2) * row_total[...]

    def result(c, carry):
        col_out[c] = bias_all[ITERS - 1, c, PIECES:, :]
        return carry

    lax.fori_loop(0, n_row, result, 0)

    for d in range(1, n_col):
        x_copy(along_col(d), me_col).wait_send()
        w_copy(along_col(d), me_col).wait_send()
        for it in range(ITERS):
            r_copy(it, along_col(d), me_col).wait_send()

    def sent(d, carry):
        y_copy(along_row(d), me_row).wait_send()
        for it in range(ITERS):
            c_copy(it, along_row(d), me_row).wait_send()
            b_copy(it, along_row(d), me_row).wait_send()
        return carry

    lax.fori_loop(1, n_row, sent, 0)


def per_device(
    n_row,
    n_col,
    samples,
    sample_logw,
    references,
    reference_logw,
    dual_start,
    kept_tiles,
    tile_counts,
):
    own_blocks = samples.shape[0] // TILE
    row_blocks = own_blocks * n_col
    dim = samples.shape[1]
    n_slot = kept_tiles.shape[2]
    tiles = kept_tiles[0, 0]
    used = jnp.arange(n_slot, dtype=jnp.int32) < tile_counts[0, 0]
    col_ids = jnp.where(used, tiles % n_row, -1)
    row_ids = jnp.where(used, tiles // n_row, -1)
    x_own = samples.reshape(own_blocks, TILE, dim).transpose(0, 2, 1)
    f32 = jnp.float32
    bf16 = jnp.bfloat16
    dma = pltpu.SemaphoreType.DMA
    vmem = pltpu.VMEM
    row_dual, col_dual = pl.pallas_call(
        functools.partial(kernel, n_row, n_col),
        out_shape=(
            jax.ShapeDtypeStruct((row_blocks, PIECES, LANES), f32),
            jax.ShapeDtypeStruct((n_row, PIECES, LANES), f32),
        ),
        in_specs=[pl.BlockSpec(memory_space=pltpu.SMEM)]
        + [pl.BlockSpec(memory_space=pltpu.VMEM)] * 7,
        out_specs=(pl.BlockSpec(memory_space=pltpu.VMEM),) * 2,
        scratch_shapes=[
            vmem((row_blocks, dim, TILE), f32),
            vmem((row_blocks, PIECES, LANES), f32),
            vmem((n_row, dim, TILE), f32),
            vmem((row_blocks, DEPTH, TILE), bf16),
            vmem((row_blocks, DEPTH, TILE), bf16),
            vmem((n_row, DEPTH, TILE), bf16),
            vmem((n_row, DEPTH, TILE), bf16),
            vmem((row_blocks, PIECES, LANES), f32),
            vmem((TILE, TILE), f32),
            vmem((TILE, TILE), f32),
            vmem((1, TILE), f32),
            vmem((1, TILE), f32),
            vmem((n_slot, TILE), f32),
            vmem((ITERS, n_row, PIECES, LANES), f32),
            vmem((ITERS, n_row, PIECES, LANES), f32),
            vmem((ITERS, 2 * PIECES, LANES), f32),
            vmem((ITERS, n_row, 2 * PIECES, LANES), f32),
            vmem((ITERS, row_blocks, PIECES, LANES), f32),
            vmem((ITERS, n_col, row_blocks, PIECES, LANES), f32),
            vmem((row_blocks, PIECES, LANES), f32),
            dma((n_col,)),
            dma((n_col,)),
            dma((n_col,)),
            dma((n_col,)),
            dma((n_row,)),
            dma((n_row,)),
            dma((ITERS, n_row)),
            dma((ITERS, n_row)),
            dma((ITERS, n_row)),
            dma((ITERS, n_row)),
            dma((ITERS, n_col)),
            dma((ITERS, n_col)),
        ],
        compiler_params=pltpu.CompilerParams(
            collective_id=0, has_side_effects=True, vmem_limit_bytes=48 * 2**20
        ),
        name="sinkhorn",
    )(
        tiles,
        jnp.broadcast_to(col_ids[:, None], (n_slot, TILE)),
        jnp.broadcast_to(row_ids[:, None], (n_slot, TILE)),
        x_own,
        sample_logw.reshape(own_blocks, PIECES, LANES),
        references.T,
        reference_logw.reshape(PIECES, LANES),
        dual_start.reshape(row_blocks, PIECES, LANES),
    )
    return row_dual.reshape(1, -1), col_dual.reshape(1, -1)


def solution(mesh):
    n_row, n_col = mesh.shape["row"], mesh.shape["col"]
    both = ("row", "col")
    in_specs = (
        P(both, None),
        P(both),
        P(both, None),
        P(both),
        P("row", None),
        P("row", "col", None),
        P("row", "col"),
    )
    out_specs = (P("row", None), P("col", None))
    return jax.shard_map(
        functools.partial(per_device, n_row, n_col),
        mesh=mesh,
        in_specs=in_specs,
        out_specs=out_specs,
        check_vma=False,
    )
```

```python
import functools

import jax
import jax.numpy as jnp
from jax import lax
from jax.experimental import pallas as pl
from jax.experimental.pallas import tpu as pltpu
from jax.sharding import PartitionSpec as P

TILE = 512
ITERS = 3
LANES = 128
PIECES = TILE // LANES
DEPTH = 128
BIAS = 16
SUB = 8
CHUNK = 64
AT_ONCE = 8
NX, NZ, NY = 4, 2, 4
MESH = pl.DeviceIdType.MESH

lowest = -1e30
epsilon = 0.1
LOG2E = 1.4426950408889634
LN2 = 0.6931471805599453
SCALE = 2.0 / epsilon * LOG2E


def lse(values):
    peak = jnp.max(values, axis=0, keepdims=True)
    return peak + jnp.log2(jnp.sum(jnp.exp2(values - peak), axis=0, keepdims=True))


def halves(values):
    high = values.astype(jnp.bfloat16)
    low = (values - high.astype(jnp.float32)).astype(jnp.bfloat16)
    return high, low


def place_points(points, reduced, kept, slot, at, dim):
    high, low = halves(points)
    size = points.shape[0]
    for ref, order in ((reduced, (high, high, low)), (kept, (high, low, high))):
        for k, part in enumerate(order):
            ref[slot, pl.ds(BIAS + k * dim + at, size), :] = part


def fill(reduced, kept, slot, dim):
    top = BIAS + 3 * dim
    for ref in (reduced, kept):
        ref[slot, top:, :] = jnp.zeros((DEPTH - top, TILE), jnp.bfloat16)
    kept[slot, :BIAS, :] = jnp.ones((BIAS, TILE), jnp.bfloat16)


def place_bias(rows, reduced, slot):
    index = lax.broadcasted_iota(jnp.int32, (BIAS, LANES), 0)
    for piece in range(PIECES):
        row = rows[piece : piece + 1, :]
        first = row.astype(jnp.bfloat16).astype(jnp.float32)
        rest = row - first
        second = rest.astype(jnp.bfloat16).astype(jnp.float32)
        third = rest - second
        tile = jnp.where(
            index == 0,
            first,
            jnp.where(index == 1, second, jnp.where(index == 2, third, 0.0)),
        )
        reduced[slot, :BIAS, piece * LANES : (piece + 1) * LANES] = tile.astype(jnp.bfloat16)


def cut(line):
    return [line[:, k * LANES : (k + 1) * LANES] for k in range(PIECES)]


def kernel(
    n_row,
    n_col,
    tiles,
    col_ids,
    row_ids,
    x_own,
    xw_own,
    y_own,
    yw_own,
    start,
    row_out,
    col_out,
    x_all,
    xw_all,
    y_all,
    x_reduced,
    x_kept,
    y_reduced,
    y_kept,
    x_norm,
    slots,
    col_part,
    col_recv,
    col_send,
    bias_all,
    dual_send,
    row_part,
    row_recv,
    row_total,
    x_ssem,
    x_rsem,
    w_ssem,
    w_rsem,
    y_ssem,
    y_rsem,
    c_ssem,
    c_rsem,
    b_ssem,
    b_rsem,
    g_ssem,
    g_rsem,
    r_ssem,
    r_rsem,
):
    me_row = lax.axis_index("row")
    me_col = lax.axis_index("col")
    n_slot = slots.shape[0]
    row_blocks = x_all.shape[0]
    own_blocks = x_own.shape[0]

    def along_row(d):
        return lax.rem(me_row + d, n_row)

    def along_col(d):
        return lax.rem(me_col + d, n_col)

    barrier = pltpu.get_barrier_semaphore()

    def greet(d, carry):
        pl.semaphore_signal(
            barrier, inc=1, device_id={"row": along_row(d)}, device_id_type=MESH
        )
        return carry

    lax.fori_loop(1, n_row, greet, 0)
    for d in range(1, n_col):
        pl.semaphore_signal(
            barrier, inc=1, device_id={"col": along_col(d)}, device_id_type=MESH
        )

    def fill_y(c, carry):
        fill(y_reduced, y_kept, c, y_own.shape[0])
        return carry

    def fill_x(b, carry):
        fill(x_reduced, x_kept, b, y_own.shape[0])
        return carry

    lax.fori_loop(0, n_row, fill_y, 0)
    lax.fori_loop(0, row_blocks, fill_x, 0)
    pl.semaphore_wait(barrier, n_row - 1 + n_col - 1)

    def x_copy(target, owner, turn, source):
        return pltpu.make_async_remote_copy(
            src_ref=source,
            dst_ref=x_all.at[pl.ds(owner * own_blocks, own_blocks)],
            send_sem=x_ssem.at[turn],
            recv_sem=x_rsem.at[owner],
            device_id={"col": target},
            device_id_type=MESH,
        )

    def w_copy(target, owner):
        return pltpu.make_async_remote_copy(
            src_ref=xw_own,
            dst_ref=xw_all.at[pl.ds(owner * own_blocks, own_blocks)],
            send_sem=w_ssem.at[target],
            recv_sem=w_rsem.at[owner],
            device_id={"col": target},
            device_id_type=MESH,
        )

    def y_copy(target, owner, first, count, source=None):
        rows = pl.ds(first * SUB, count * SUB)
        return pltpu.make_async_remote_copy(
            src_ref=y_all.at[owner, rows] if source is None else source.at[rows],
            dst_ref=y_all.at[owner, rows],
            send_sem=y_ssem,
            recv_sem=y_rsem.at[owner, first],
            device_id={"row": target},
            device_id_type=MESH,
        )

    def c_copy(it, target, owner):
        return pltpu.make_async_remote_copy(
            src_ref=col_part.at[it, target],
            dst_ref=col_recv.at[it, owner],
            send_sem=c_ssem.at[it, target],
            recv_sem=c_rsem.at[it, owner],
            device_id={"row": target},
            device_id_type=MESH,
        )

    def b_copy(it, target, owner):
        return pltpu.make_async_remote_copy(
            src_ref=col_send.at[it],
            dst_ref=bias_all.at[it, owner],
            send_sem=b_ssem.at[it, target],
            recv_sem=b_rsem.at[it, owner],
            device_id={"row": target},
            device_id_type=MESH,
        )

    def g_copy(target, owner):
        return pltpu.make_async_remote_copy(
            src_ref=dual_send,
            dst_ref=col_out.at[owner],
            send_sem=g_ssem.at[target],
            recv_sem=g_rsem.at[owner],
            device_id={"row": target},
            device_id_type=MESH,
        )

    def r_copy(it, target, owner):
        return pltpu.make_async_remote_copy(
            src_ref=row_part.at[it],
            dst_ref=row_recv.at[it, owner],
            send_sem=r_ssem.at[it, target],
            recv_sem=r_rsem.at[it, owner],
            device_id={"col": target},
            device_id_type=MESH,
        )

    dim = y_own.shape[0]
    groups = dim // SUB
    half = groups // 2
    at_x = lax.rem(me_row, NX)
    at_z = lax.rem(lax.div(me_row, NX), NZ)
    at_y = lax.div(me_row, NX * NZ)

    def shifted(axis, shift, other, z):
        steps = (shift, other) if axis == 0 else (other, shift)
        return (
            lax.rem(at_y + steps[1], NY) * (NX * NZ)
            + lax.rem(at_z + z, NZ) * NX
            + lax.rem(at_x + steps[0], NX)
        )

    def ring(axis, step):
        return shifted(axis, step, 0, 0)

    forward, back = 1, NX - 1

    def send_half(axis, part, owner, source=None):
        for step in (forward, back):
            y_copy(ring(axis, step), owner, part * half, half, source).start()

    def relay(axis, part, owner, step):
        y_copy(me_row, owner, part * half, half).wait_recv()
        piece = part * half + (0 if step == forward else half // 2)
        y_copy(ring(axis, step), owner, piece, half // 2).start()

    def arrive(part, owner):
        for piece in range(2):
            y_copy(me_row, owner, part * half + piece * (half // 2), half // 2).wait_recv()

    def place_y(part, owner):
        at = part * half * SUB
        points = y_all[owner, at : at + half * SUB, :]
        place_points(points, y_reduced, y_kept, owner, at, dim)

    partner = shifted(0, 0, 0, 1)
    y_copy(partner, me_row, 0, groups, y_own).start()
    for part in range(2):
        send_half(part, part, me_row, y_own)
    beside = me_col + 1 - 2 * lax.rem(me_col, 2)
    across = me_col + 2 - 4 * lax.rem(lax.div(me_col, 2), 2)
    if n_col > 1:
        x_copy(beside, me_col, 0, x_own).start()
    if n_col > 2:
        x_copy(across, me_col, 1, x_own).start()
    for d in range(1, n_col):
        w_copy(along_col(d), me_col).start()

    y_norm = jnp.sum(y_own[...] * y_own[...], axis=0, keepdims=True)
    y_all[me_row] = y_own[...]
    for d in range(own_blocks):
        x_all[me_col * own_blocks + d] = x_own[d]
        xw_all[me_col * own_blocks + d] = xw_own[d]

    y_copy(me_row, partner, 0, groups).wait_recv()
    for part in range(2):
        send_half(part, part, partner)
    for z in range(NZ):
        for part in range(2):
            for step in (forward, back):
                relay(part, part, shifted(part, NX - step, 0, z), step)
    for part in range(2):
        for z in range(NZ):
            owner = shifted(part, 0, 0, z)
            send_half(1 - part, part, owner, y_own if z == 0 else None)
            for shift in (forward, back):
                send_half(1 - part, part, shifted(part, shift, 0, z))
    for part in range(2):
        for z in range(NZ):
            owner = shifted(part, 2, 0, z)
            arrive(part, owner)
            send_half(1 - part, part, owner)
    if n_col > 2:
        x_copy(me_col, across, 0, x_own).wait_recv()
        relayed = x_all.at[pl.ds(across * own_blocks, own_blocks)]
        x_copy(beside, across, 2, relayed).start()
    for part in range(2):
        for shift in range(NX):
            for z in range(NZ):
                place_y(part, shifted(part, shift, 0, z))

    for shift in (0, 1, 3, 2):
        for z in range(NZ):
            for part in range(2):
                for step in (forward, back):
                    owner = shifted(part, shift, NY - step, z)
                    relay(1 - part, part, owner, step)
                    place_y(part, owner)

    if n_col > 1:
        x_copy(me_col, beside, 0, x_own).wait_recv()
    if n_col > 2:
        last = across + 1 - 2 * lax.rem(across, 2)
        x_copy(me_col, last, 0, x_own).wait_recv()
    for d in range(1, n_col):
        w_copy(me_col, along_col(d)).wait_recv()

    def x_block(b, carry):
        points = x_all[b]
        place_points(points * SCALE, x_reduced, x_kept, b, 0, dim)
        norm = cut(jnp.sum(points * points, axis=0, keepdims=True))
        for k in range(PIECES):
            x_norm[b, k : k + 1, :] = norm[k]
        bias = xw_all[b] + (start[b] - x_norm[b]) * (1.0 / epsilon)
        place_bias(bias * LOG2E, x_reduced, b)
        return carry

    lax.fori_loop(0, row_blocks, x_block, 0)

    for shift in (0, 1, 3, 2):
        for z in range(NZ):
            for part in range(2):
                owner = shifted(part, shift, 2, z)
                arrive(part, owner)
                place_y(part, owner)

    def visit(reduced, kept, by_column):
        def one(slot):
            tile = tiles[slot]
            row = lax.div(tile, n_row)
            col = lax.rem(tile, n_row)
            left, right = (row, col) if by_column else (col, row)
            score = lax.dot_general(
                reduced[left],
                kept[right],
                (((0,), (0,)), ((), ())),
                preferred_element_type=jnp.float32,
            )
            peaks, sums = [], []
            for at in range(0, TILE, CHUNK):
                part = score[at : at + CHUNK].reshape(CHUNK // SUB, SUB, TILE)
                peak = jnp.max(part, axis=0)
                peaks.append(peak)
                sums.append(jnp.sum(jnp.exp2(part - peak[None]), axis=0))
            top = functools.reduce(jnp.maximum, peaks)
            total = sum(a * jnp.exp2(b - top) for a, b in zip(sums, peaks))
            highest = jnp.max(top, axis=0, keepdims=True)
            total = jnp.sum(total * jnp.exp2(top - highest), axis=0, keepdims=True)
            slots[pl.ds(slot, 1), :] = highest + jnp.log2(total)

        def several(i, carry):
            for k in range(AT_ONCE):
                one(i * AT_ONCE + k)
            return carry

        lax.fori_loop(0, n_slot // AT_ONCE, several, 0)

    def fold(ids, block):
        return cut(lse(jnp.where(ids[...] == block, slots[...], lowest)))

    def iteration(it, carry):
        visit(x_reduced, y_kept, True)

        def col_fold(c, inner):
            line = fold(col_ids, c)
            for k in range(PIECES):
                col_part[it, c, k : k + 1, :] = line[k]
            return inner

        lax.fori_loop(0, n_row, col_fold, 0, unroll=4)

        def c_start(d, inner):
            c_copy(it, along_row(d), me_row).start()
            return inner

        lax.fori_loop(1, n_row, c_start, 0)
        col_recv[it, me_row] = col_part[it, me_row]

        def c_wait(d, inner):
            c_copy(it, me_row, along_row(d)).wait_recv()
            return inner

        lax.fori_loop(1, n_row, c_wait, 0)
        total = lse(col_recv[it])[0]
        bias = yw_own[...] * LOG2E - total
        norm = cut(y_norm)
        col_send[it] = bias
        for k in range(PIECES):
            dual_send[k : k + 1, :] = norm[k] - (epsilon * LN2) * total[k : k + 1]

        def b_start(d, inner):
            b_copy(it, along_row(d), me_row).start()
            return inner

        lax.fori_loop(1, n_row, b_start, 0)

        def g_start(d, inner):
            g_copy(along_row(d), me_row).start()
            return inner

        @pl.when(it == ITERS - 1)
        def _():
            lax.fori_loop(1, n_row, g_start, 0)
            col_out[me_row] = dual_send[...]

        place_bias(bias, y_reduced, me_row)

        def b_wait(d, inner):
            owner = along_row(d)
            b_copy(it, me_row, owner).wait_recv()
            place_bias(bias_all[it, owner], y_reduced, owner)
            return inner

        lax.fori_loop(1, n_row, b_wait, 0)

        visit(y_reduced, x_kept, False)

        def row_fold(b, inner):
            line = fold(row_ids, b)
            for k in range(PIECES):
                row_part[it, b, k : k + 1, :] = line[k]
            return inner

        lax.fori_loop(0, row_blocks, row_fold, 0, unroll=4)
        for d in range(1, n_col):
            r_copy(it, along_col(d), me_col).start()
        row_recv[it, me_col] = row_part[it]
        for d in range(1, n_col):
            r_copy(it, me_col, along_col(d)).wait_recv()
        row_total[...] = lse(row_recv[it])[0]

        def row_bias(b, inner):
            place_bias(xw_all[b] * LOG2E - row_total[b], x_reduced, b)
            return inner

        lax.fori_loop(0, row_blocks, row_bias, 0)
        return carry

    lax.fori_loop(0, ITERS, iteration, 0)

    row_out[...] = x_norm[...] - (epsilon * LN2) * row_total[...]

    def result(d, carry):
        g_copy(me_row, along_row(d)).wait_recv()
        return carry

    lax.fori_loop(1, n_row, result, 0)

    for d in range(1, n_col):
        w_copy(along_col(d), me_col).wait_send()
        for it in range(ITERS):
            r_copy(it, along_col(d), me_col).wait_send()

    for turn in range(min(n_col - 1, 3)):
        x_copy(beside, me_col, turn, x_own).wait_send()
    pltpu.make_async_remote_copy(
        src_ref=y_all.at[pl.ds(0, n_row - 1)],
        dst_ref=y_all.at[pl.ds(0, n_row - 1)],
        send_sem=y_ssem,
        recv_sem=y_rsem.at[0, 0],
        device_id={"row": partner},
        device_id_type=MESH,
    ).wait_send()

    def sent(d, carry):
        g_copy(along_row(d), me_row).wait_send()
        for it in range(ITERS):
            c_copy(it, along_row(d), me_row).wait_send()
            b_copy(it, along_row(d), me_row).wait_send()
        return carry

    lax.fori_loop(1, n_row, sent, 0)


def per_device(
    n_row,
    n_col,
    samples,
    sample_logw,
    references,
    reference_logw,
    dual_start,
    kept_tiles,
    tile_counts,
):
    own_blocks = samples.shape[0] // TILE
    row_blocks = own_blocks * n_col
    dim = samples.shape[1]
    n_slot = kept_tiles.shape[2]
    tiles = kept_tiles[0, 0]
    used = jnp.arange(n_slot, dtype=jnp.int32) < tile_counts[0, 0]
    col_ids = jnp.where(used, tiles % n_row, -1)
    row_ids = jnp.where(used, tiles // n_row, -1)
    x_own = samples.reshape(own_blocks, TILE, dim).transpose(0, 2, 1)
    f32 = jnp.float32
    bf16 = jnp.bfloat16
    dma = pltpu.SemaphoreType.DMA
    vmem = pltpu.VMEM
    row_dual, col_dual = pl.pallas_call(
        functools.partial(kernel, n_row, n_col),
        out_shape=(
            jax.ShapeDtypeStruct((row_blocks, PIECES, LANES), f32),
            jax.ShapeDtypeStruct((n_row, PIECES, LANES), f32),
        ),
        in_specs=[pl.BlockSpec(memory_space=pltpu.SMEM)]
        + [pl.BlockSpec(memory_space=pltpu.VMEM)] * 7,
        out_specs=(pl.BlockSpec(memory_space=pltpu.VMEM),) * 2,
        scratch_shapes=[
            vmem((row_blocks, dim, TILE), f32),
            vmem((row_blocks, PIECES, LANES), f32),
            vmem((n_row, dim, TILE), f32),
            vmem((row_blocks, DEPTH, TILE), bf16),
            vmem((row_blocks, DEPTH, TILE), bf16),
            vmem((n_row, DEPTH, TILE), bf16),
            vmem((n_row, DEPTH, TILE), bf16),
            vmem((row_blocks, PIECES, LANES), f32),
            vmem((n_slot, TILE), f32),
            vmem((ITERS, n_row, PIECES, LANES), f32),
            vmem((ITERS, n_row, PIECES, LANES), f32),
            vmem((ITERS, PIECES, LANES), f32),
            vmem((ITERS, n_row, PIECES, LANES), f32),
            vmem((PIECES, LANES), f32),
            vmem((ITERS, row_blocks, PIECES, LANES), f32),
            vmem((ITERS, n_col, row_blocks, PIECES, LANES), f32),
            vmem((row_blocks, PIECES, LANES), f32),
            dma((3,)),
            dma((n_col,)),
            dma((n_col,)),
            dma((n_col,)),
            dma,
            dma((n_row, dim // SUB)),
            dma((ITERS, n_row)),
            dma((ITERS, n_row)),
            dma((ITERS, n_row)),
            dma((ITERS, n_row)),
            dma((n_row,)),
            dma((n_row,)),
            dma((ITERS, n_col)),
            dma((ITERS, n_col)),
        ],
        compiler_params=pltpu.CompilerParams(
            collective_id=0, has_side_effects=True, vmem_limit_bytes=48 * 2**20
        ),
        name="sinkhorn",
    )(
        tiles,
        jnp.broadcast_to(col_ids[:, None], (n_slot, TILE)),
        jnp.broadcast_to(row_ids[:, None], (n_slot, TILE)),
        x_own,
        sample_logw.reshape(own_blocks, PIECES, LANES),
        references.T,
        reference_logw.reshape(PIECES, LANES),
        dual_start.reshape(row_blocks, PIECES, LANES),
    )
    return row_dual.reshape(1, -1), col_dual.reshape(1, -1)


def solution(mesh):
    n_row, n_col = mesh.shape["row"], mesh.shape["col"]
    both = ("row", "col")
    in_specs = (
        P(both, None),
        P(both),
        P(both, None),
        P(both),
        P("row", None),
        P("row", "col", None),
        P("row", "col"),
    )
    out_specs = (P("row", None), P("col", None))
    return jax.shard_map(
        functools.partial(per_device, n_row, n_col),
        mesh=mesh,
        in_specs=in_specs,
        out_specs=out_specs,
        check_vma=False,
    )
```

```python
import functools

import jax
import jax.numpy as jnp
from jax import lax
from jax.experimental import pallas as pl
from jax.experimental.pallas import tpu as pltpu
from jax.sharding import PartitionSpec as P

TILE = 512
ITERS = 3
LANES = 128
PIECES = TILE // LANES
DEPTH = 128
BIAS = 16
SUB = 8
CHUNK = 64
AT_ONCE = 8
NX, NZ, NY = 4, 2, 4
MESH = pl.DeviceIdType.MESH

lowest = -1e30
epsilon = 0.1
LOG2E = 1.4426950408889634
LN2 = 0.6931471805599453
SCALE = 2.0 / epsilon * LOG2E


def lse(values):
    peak = jnp.max(values, axis=0, keepdims=True)
    return peak + jnp.log2(jnp.sum(jnp.exp2(values - peak), axis=0, keepdims=True))


def halves(values):
    high = values.astype(jnp.bfloat16)
    low = (values - high.astype(jnp.float32)).astype(jnp.bfloat16)
    return high, low


def place_points(points, reduced, kept, slot, at, dim):
    high, low = halves(points)
    size = points.shape[0]
    for ref, order in ((reduced, (high, high, low)), (kept, (high, low, high))):
        for k, part in enumerate(order):
            ref[slot, pl.ds(BIAS + k * dim + at, size), :] = part


def fill(reduced, kept, slot, dim):
    top = BIAS + 3 * dim
    for ref in (reduced, kept):
        ref[slot, top:, :] = jnp.zeros((DEPTH - top, TILE), jnp.bfloat16)
    kept[slot, :BIAS, :] = jnp.ones((BIAS, TILE), jnp.bfloat16)


def place_bias(rows, reduced, slot):
    index = lax.broadcasted_iota(jnp.int32, (BIAS, LANES), 0)
    for piece in range(PIECES):
        row = rows[piece : piece + 1, :]
        first = row.astype(jnp.bfloat16).astype(jnp.float32)
        rest = row - first
        second = rest.astype(jnp.bfloat16).astype(jnp.float32)
        third = rest - second
        tile = jnp.where(
            index == 0,
            first,
            jnp.where(index == 1, second, jnp.where(index == 2, third, 0.0)),
        )
        reduced[slot, :BIAS, piece * LANES : (piece + 1) * LANES] = tile.astype(jnp.bfloat16)


def cut(line):
    return [line[:, k * LANES : (k + 1) * LANES] for k in range(PIECES)]


def kernel(
    n_row,
    n_col,
    tiles,
    count,
    x_in,
    xw_in,
    y_in,
    yw_in,
    start_in,
    row_out,
    col_out,
    x_own,
    xw_own,
    y_own,
    yw_own,
    start,
    col_ids,
    row_ids,
    x_all,
    xw_all,
    y_all,
    x_reduced,
    x_kept,
    y_reduced,
    y_kept,
    x_norm,
    slots,
    col_part,
    col_recv,
    col_send,
    bias_all,
    dual_send,
    row_part,
    row_recv,
    row_total,
    in_sem,
    x_ssem,
    x_rsem,
    w_ssem,
    w_rsem,
    y_ssem,
    y_rsem,
    c_ssem,
    c_rsem,
    b_ssem,
    b_rsem,
    g_ssem,
    g_rsem,
    r_ssem,
    r_rsem,
):
    me_row = lax.axis_index("row")
    me_col = lax.axis_index("col")
    n_slot = slots.shape[0]
    row_blocks = x_all.shape[0]
    own_blocks = x_own.shape[0]

    def bytes_of(ref, send_sem, recv_sem, axis):
        peer = along_row(1) if axis == "row" else along_col(1)
        return pltpu.make_async_remote_copy(
            src_ref=ref,
            dst_ref=ref,
            send_sem=send_sem,
            recv_sem=recv_sem,
            device_id={axis: peer},
            device_id_type=MESH,
        )

    def along_row(d):
        return lax.rem(me_row + d, n_row)

    def along_col(d):
        return lax.rem(me_col + d, n_col)

    barrier = pltpu.get_barrier_semaphore()
    fetches = [
        pltpu.make_async_copy(y_in, y_own, in_sem.at[0]),
        pltpu.make_async_copy(xw_in, xw_own, in_sem.at[1]),
        pltpu.make_async_copy(yw_in, yw_own, in_sem.at[2]),
        pltpu.make_async_copy(start_in, start, in_sem.at[3]),
    ] + [
        pltpu.make_async_copy(x_in.at[:, pl.ds(k * TILE, TILE)], x_own.at[k], in_sem.at[4 + k])
        for k in range(own_blocks)
    ]
    for fetch in fetches:
        fetch.start()

    def greet(d, carry):
        pl.semaphore_signal(
            barrier, inc=1, device_id={"row": along_row(d)}, device_id_type=MESH
        )
        return carry

    lax.fori_loop(1, n_row, greet, 0)
    for d in range(1, n_col):
        pl.semaphore_signal(
            barrier, inc=1, device_id={"col": along_col(d)}, device_id_type=MESH
        )

    def fill_y(c, carry):
        fill(y_reduced, y_kept, c, y_own.shape[0])
        return carry

    def fill_x(b, carry):
        fill(x_reduced, x_kept, b, y_own.shape[0])
        return carry

    lax.fori_loop(0, n_row, fill_y, 0)
    lax.fori_loop(0, row_blocks, fill_x, 0)
    index = lax.broadcasted_iota(jnp.int32, (n_slot, TILE), 0)

    def name_slot(k, ids):
        tile = tiles[0, 0, k]
        used = k < count[0, 0]
        row = jnp.where(used, lax.div(tile, n_row), -1)
        col = jnp.where(used, lax.rem(tile, n_row), -1)
        return (jnp.where(index == k, row, ids[0]), jnp.where(index == k, col, ids[1]))

    row_names, col_names = lax.fori_loop(0, n_slot, name_slot, (index, index))
    row_ids[...] = row_names
    col_ids[...] = col_names
    for fetch in fetches:
        fetch.wait()
    pl.semaphore_wait(barrier, n_row - 1 + n_col - 1)

    def x_copy(target, owner, turn, source):
        return pltpu.make_async_remote_copy(
            src_ref=source,
            dst_ref=x_all.at[pl.ds(owner * own_blocks, own_blocks)],
            send_sem=x_ssem.at[turn],
            recv_sem=x_rsem.at[owner],
            device_id={"col": target},
            device_id_type=MESH,
        )

    def w_copy(target, owner):
        return pltpu.make_async_remote_copy(
            src_ref=xw_own,
            dst_ref=xw_all.at[pl.ds(owner * own_blocks, own_blocks)],
            send_sem=w_ssem,
            recv_sem=w_rsem,
            device_id={"col": target},
            device_id_type=MESH,
        )

    def y_copy(target, owner, first, size, mark, source=None):
        rows = pl.ds(first * SUB, size * SUB)
        return pltpu.make_async_remote_copy(
            src_ref=y_all.at[owner, rows] if source is None else source.at[rows],
            dst_ref=y_all.at[owner, rows],
            send_sem=y_ssem,
            recv_sem=y_rsem.at[mark],
            device_id={"row": target},
            device_id_type=MESH,
        )

    def c_copy(it, target, owner):
        return pltpu.make_async_remote_copy(
            src_ref=col_part.at[it, target],
            dst_ref=col_recv.at[it, owner],
            send_sem=c_ssem.at[it],
            recv_sem=c_rsem.at[it],
            device_id={"row": target},
            device_id_type=MESH,
        )

    def b_copy(it, target, owner, mark):
        return pltpu.make_async_remote_copy(
            src_ref=col_send.at[it],
            dst_ref=bias_all.at[it, owner],
            send_sem=b_ssem.at[it],
            recv_sem=b_rsem.at[it, mark],
            device_id={"row": target},
            device_id_type=MESH,
        )

    def g_copy(target, owner):
        return pltpu.make_async_remote_copy(
            src_ref=dual_send,
            dst_ref=col_out.at[owner],
            send_sem=g_ssem,
            recv_sem=g_rsem,
            device_id={"row": target},
            device_id_type=MESH,
        )

    def r_copy(it, target, owner):
        return pltpu.make_async_remote_copy(
            src_ref=row_part.at[it],
            dst_ref=row_recv.at[it, owner],
            send_sem=r_ssem.at[it],
            recv_sem=r_rsem.at[it],
            device_id={"col": target},
            device_id_type=MESH,
        )

    dim = y_own.shape[0]
    groups = dim // SUB
    half = groups // 2
    at_x = lax.rem(me_row, NX)
    at_z = lax.rem(lax.div(me_row, NX), NZ)
    at_y = lax.div(me_row, NX * NZ)

    def shifted(axis, shift, other, z):
        steps = (shift, other) if axis == 0 else (other, shift)
        return (
            lax.rem(at_y + steps[1], NY) * (NX * NZ)
            + lax.rem(at_z + z, NZ) * NX
            + lax.rem(at_x + steps[0], NX)
        )

    def ring(axis, step):
        return shifted(axis, step, 0, 0)

    forward, back = 1, NX - 1

    def near_first(part, turn, z):
        return 1 + (part * 2 + turn) * NZ + z

    def far_first(part):
        return 1 + 4 * NZ + part

    def near_second(part, turn, shift, z):
        return 3 + 4 * NZ + ((part * 2 + turn) * NX + shift) * NZ + z

    def far_second(part, shift):
        return 3 + 4 * NZ + 4 * NX * NZ + part * NX + shift

    def send_half(axis, part, owner, mark, source=None):
        for turn, step in enumerate((forward, back)):
            y_copy(ring(axis, step), owner, part * half, half, mark(turn), source).start()

    def relay(axis, part, owner, turn, mark, far):
        y_copy(me_row, owner, part * half, half, mark).wait_recv()
        piece = part * half + turn * (half // 2)
        step = (forward, back)[turn]
        y_copy(ring(axis, step), owner, piece, half // 2, far).start()

    def arrive(mark):
        bytes_of(y_all.at[0], y_ssem, y_rsem.at[mark], "row").wait_recv()

    def place_y(part, owner):
        at = part * half * SUB
        points = y_all[owner, at : at + half * SUB, :]
        place_points(points, y_reduced, y_kept, owner, at, dim)

    def first(part, owner, z, source=None):
        send_half(part, part, owner, lambda turn: near_first(part, turn, z), source)

    def second(part, owner, shift, z, source=None):
        mark = lambda turn: near_second(part, turn, shift, z)
        send_half(1 - part, part, owner, mark, source)

    partner = shifted(0, 0, 0, 1)
    steps = [(y, z, x) for y in range(NY) for z in range(NZ) for x in range(NX)]
    steps = sorted(steps, key=lambda s: -(min(s[0], NY - s[0]) + s[1] + min(s[2], NX - s[2])))
    peers = [(shifted(0, x, y, z), (NY - y) % NY) for y, z, x in steps[:-1]]
    far_cols = (2, 1, 3)[-(n_col - 1) :] if n_col > 1 else ()
    y_copy(partner, me_row, 0, groups, 0, y_own).start()
    for part in range(2):
        first(part, me_row, 0, y_own)
    beside = me_col + 1 - 2 * lax.rem(me_col, 2)
    across = me_col + 2 - 4 * lax.rem(lax.div(me_col, 2), 2)
    if n_col > 1:
        x_copy(beside, me_col, 0, x_own).start()
    if n_col > 2:
        x_copy(across, me_col, 1, x_own).start()
    for part in range(2):
        second(part, me_row, 0, 0, y_own)
    for d in range(1, n_col):
        w_copy(along_col(d), me_col).start()

    y_norm = jnp.sum(y_own[...] * y_own[...], axis=0, keepdims=True)
    y_all[me_row] = y_own[...]
    for d in range(own_blocks):
        x_all[me_col * own_blocks + d] = x_own[d]
        xw_all[me_col * own_blocks + d] = xw_own[d]

    y_copy(me_row, partner, 0, groups, 0).wait_recv()
    for part in range(2):
        first(part, partner, 1)
    for z in range(NZ):
        for part in range(2):
            for turn, step in enumerate((forward, back)):
                owner = shifted(part, NX - step, 0, z)
                relay(part, part, owner, turn, near_first(part, turn, z), far_first(part))
    for part in range(2):
        second(part, partner, 0, 1)
        for z in range(NZ):
            for shift in (forward, back):
                second(part, shifted(part, shift, 0, z), shift, z)
    for part in range(2):
        arrive(far_first(part))
        for z in range(NZ):
            second(part, shifted(part, 2, 0, z), 2, z)
    if n_col > 2:
        x_copy(me_col, across, 0, x_own).wait_recv()
        relayed = x_all.at[pl.ds(across * own_blocks, own_blocks)]
        x_copy(beside, across, 2, relayed).start()
    for part in range(2):
        for shift in range(NX):
            for z in range(NZ):
                place_y(part, shifted(part, shift, 0, z))

    for shift in (0, 1, 3, 2):
        for z in range(NZ):
            for part in range(2):
                for turn, step in enumerate((forward, back)):
                    owner = shifted(part, shift, NY - step, z)
                    near = near_second(part, turn, shift, z)
                    relay(1 - part, part, owner, turn, near, far_second(part, shift))
                    place_y(part, owner)

    if n_col > 1:
        x_copy(me_col, beside, 0, x_own).wait_recv()
    if n_col > 2:
        last = across + 1 - 2 * lax.rem(across, 2)
        x_copy(me_col, last, 0, x_own).wait_recv()
    if n_col > 1:
        others = xw_all.at[pl.ds(0, (n_col - 1) * own_blocks)]
        bytes_of(others, w_ssem, w_rsem, "col").wait_recv()

    def x_block(b, carry):
        points = x_all[b]
        place_points(points * SCALE, x_reduced, x_kept, b, 0, dim)
        norm = cut(jnp.sum(points * points, axis=0, keepdims=True))
        for k in range(PIECES):
            x_norm[b, k : k + 1, :] = norm[k]
        bias = xw_all[b] + (start[b] - x_norm[b]) * (1.0 / epsilon)
        place_bias(bias * LOG2E, x_reduced, b)
        return carry

    lax.fori_loop(0, row_blocks, x_block, 0)

    for shift in (0, 1, 3, 2):
        for part in range(2):
            arrive(far_second(part, shift))
            for z in range(NZ):
                place_y(part, shifted(part, shift, 2, z))

    def visit(reduced, kept, by_column):
        def one(slot):
            tile = tiles[0, 0, slot]
            row = lax.div(tile, n_row)
            col = lax.rem(tile, n_row)
            left, right = (row, col) if by_column else (col, row)
            score = lax.dot_general(
                reduced[left],
                kept[right],
                (((0,), (0,)), ((), ())),
                preferred_element_type=jnp.float32,
            )
            peaks, sums = [], []
            for at in range(0, TILE, CHUNK):
                part = score[at : at + CHUNK].reshape(CHUNK // SUB, SUB, TILE)
                peak = jnp.max(part, axis=0)
                peaks.append(peak)
                sums.append(jnp.sum(jnp.exp2(part - peak[None]), axis=0))
            top = functools.reduce(jnp.maximum, peaks)
            total = sum(a * jnp.exp2(b - top) for a, b in zip(sums, peaks))
            highest = jnp.max(top, axis=0, keepdims=True)
            total = jnp.sum(total * jnp.exp2(top - highest), axis=0, keepdims=True)
            slots[pl.ds(slot, 1), :] = highest + jnp.log2(total)

        def several(i, carry):
            for k in range(AT_ONCE):
                one(i * AT_ONCE + k)
            return carry

        lax.fori_loop(0, n_slot // AT_ONCE, several, 0)

    def fold(ids, block):
        return cut(lse(jnp.where(ids[...] == block, slots[...], lowest)))

    def iteration(it, carry):
        visit(x_reduced, y_kept, True)

        def col_fold(c, inner):
            line = fold(col_ids, c)
            for k in range(PIECES):
                col_part[it, c, k : k + 1, :] = line[k]
            return inner

        lax.fori_loop(0, n_row, col_fold, 0, unroll=4)

        for target, _ in peers:
            c_copy(it, target, me_row).start()
        col_recv[it, me_row] = col_part[it, me_row]

        others = col_recv.at[it, pl.ds(0, n_row - 1)]
        bytes_of(others, c_ssem.at[it], c_rsem.at[it], "row").wait_recv()
        total = lse(col_recv[it])[0]
        bias = yw_own[...] * LOG2E - total
        norm = cut(y_norm)
        col_send[it] = bias
        for k in range(PIECES):
            dual_send[k : k + 1, :] = norm[k] - (epsilon * LN2) * total[k : k + 1]

        for target, mark in peers:
            b_copy(it, target, me_row, mark).start()

        def g_start(d, inner):
            g_copy(along_row(d), me_row).start()
            return inner

        @pl.when(it == ITERS - 1)
        def _():
            lax.fori_loop(1, n_row, g_start, 0)
            col_out[me_row] = dual_send[...]

        place_bias(bias, y_reduced, me_row)

        for offset in (0, 1, 3, 2):
            size = NZ * NX - (offset == 0)
            group = bias_all.at[it, pl.ds(0, size)]
            bytes_of(group, b_ssem.at[it], b_rsem.at[it, offset], "row").wait_recv()
            for z in range(NZ):
                for x in range(NX):
                    if offset + z + x > 0:
                        owner = shifted(0, x, offset, z)
                        place_bias(bias_all[it, owner], y_reduced, owner)

        visit(y_reduced, x_kept, False)

        def row_fold(b, inner):
            line = fold(row_ids, b)
            for k in range(PIECES):
                row_part[it, b, k : k + 1, :] = line[k]
            return inner

        lax.fori_loop(0, row_blocks, row_fold, 0, unroll=4)
        for d in far_cols:
            r_copy(it, along_col(d), me_col).start()
        row_recv[it, me_col] = row_part[it]
        if n_col > 1:
            others = row_recv.at[it, pl.ds(0, n_col - 1)]
            bytes_of(others, r_ssem.at[it], r_rsem.at[it], "col").wait_recv()
        row_total[...] = lse(row_recv[it])[0]

        def row_bias(b, inner):
            place_bias(xw_all[b] * LOG2E - row_total[b], x_reduced, b)
            return inner

        lax.fori_loop(0, row_blocks, row_bias, 0)
        return carry

    lax.fori_loop(0, ITERS, iteration, 0)

    row_out[...] = x_norm[...] - (epsilon * LN2) * row_total[...]

    others = col_out.at[pl.ds(0, n_row - 1)]
    bytes_of(others, g_ssem, g_rsem, "row").wait_recv()
    bytes_of(others, g_ssem, g_rsem, "row").wait_send()
    for turn in range(min(n_col - 1, 3)):
        x_copy(beside, me_col, turn, x_own).wait_send()
    others = y_all.at[pl.ds(0, n_row - 1)]
    bytes_of(others, y_ssem, y_rsem.at[0], "row").wait_send()
    if n_col > 1:
        others = xw_all.at[pl.ds(0, (n_col - 1) * own_blocks)]
        bytes_of(others, w_ssem, w_rsem, "col").wait_send()
    for it in range(ITERS):
        others = col_recv.at[it, pl.ds(0, n_row - 1)]
        bytes_of(others, c_ssem.at[it], c_rsem.at[it], "row").wait_send()
        others = bias_all.at[it, pl.ds(0, n_row - 1)]
        bytes_of(others, b_ssem.at[it], b_rsem.at[it, 0], "row").wait_send()
        if n_col > 1:
            others = row_recv.at[it, pl.ds(0, n_col - 1)]
            bytes_of(others, r_ssem.at[it], r_rsem.at[it], "col").wait_send()


def per_device(
    n_row,
    n_col,
    samples,
    sample_logw,
    references,
    reference_logw,
    dual_start,
    kept_tiles,
    tile_counts,
):
    own_blocks = samples.shape[0] // TILE
    row_blocks = own_blocks * n_col
    dim = samples.shape[1]
    n_slot = kept_tiles.shape[2]
    f32 = jnp.float32
    bf16 = jnp.bfloat16
    dma = pltpu.SemaphoreType.DMA
    vmem = pltpu.VMEM
    row_dual, col_dual = pl.pallas_call(
        functools.partial(kernel, n_row, n_col),
        out_shape=(
            jax.ShapeDtypeStruct((row_blocks, PIECES, LANES), f32),
            jax.ShapeDtypeStruct((n_row, PIECES, LANES), f32),
        ),
        in_specs=[pl.BlockSpec(memory_space=pltpu.SMEM)] * 2
        + [pl.BlockSpec(memory_space=pltpu.HBM)] * 5,
        out_specs=(pl.BlockSpec(memory_space=pltpu.VMEM),) * 2,
        scratch_shapes=[
            vmem((own_blocks, dim, TILE), f32),
            vmem((own_blocks, PIECES, LANES), f32),
            vmem((dim, TILE), f32),
            vmem((PIECES, LANES), f32),
            vmem((row_blocks, PIECES, LANES), f32),
            vmem((n_slot, TILE), jnp.int32),
            vmem((n_slot, TILE), jnp.int32),
            vmem((row_blocks, dim, TILE), f32),
            vmem((row_blocks, PIECES, LANES), f32),
            vmem((n_row, dim, TILE), f32),
            vmem((row_blocks, DEPTH, TILE), bf16),
            vmem((row_blocks, DEPTH, TILE), bf16),
            vmem((n_row, DEPTH, TILE), bf16),
            vmem((n_row, DEPTH, TILE), bf16),
            vmem((row_blocks, PIECES, LANES), f32),
            vmem((n_slot, TILE), f32),
            vmem((ITERS, n_row, PIECES, LANES), f32),
            vmem((ITERS, n_row, PIECES, LANES), f32),
            vmem((ITERS, PIECES, LANES), f32),
            vmem((ITERS, n_row, PIECES, LANES), f32),
            vmem((PIECES, LANES), f32),
            vmem((ITERS, row_blocks, PIECES, LANES), f32),
            vmem((ITERS, n_col, row_blocks, PIECES, LANES), f32),
            vmem((row_blocks, PIECES, LANES), f32),
            dma((4 + own_blocks,)),
            dma((3,)),
            dma((n_col,)),
            dma,
            dma,
            dma,
            dma((3 + 4 * NZ + 4 * NX * NZ + 2 * NX,)),
            dma((ITERS,)),
            dma((ITERS,)),
            dma((ITERS,)),
            dma((ITERS, NY)),
            dma,
            dma,
            dma((ITERS,)),
            dma((ITERS,)),
        ],
        compiler_params=pltpu.CompilerParams(
            collective_id=0,
            has_side_effects=True,
            vmem_limit_bytes=67043328,
        ),
        name="sinkhorn",
    )(
        kept_tiles,
        tile_counts,
        samples.T,
        sample_logw.reshape(own_blocks, PIECES, LANES),
        references.T,
        reference_logw.reshape(PIECES, LANES),
        dual_start.reshape(row_blocks, PIECES, LANES),
    )
    return row_dual.reshape(1, -1), col_dual.reshape(1, -1)


def solution(mesh):
    n_row, n_col = mesh.shape["row"], mesh.shape["col"]
    both = ("row", "col")
    in_specs = (
        P(both, None),
        P(both),
        P(both, None),
        P(both),
        P("row", None),
        P("row", "col", None),
        P("row", "col"),
    )
    out_specs = (P("row", None), P("col", None))
    return jax.shard_map(
        functools.partial(per_device, n_row, n_col),
        mesh=mesh,
        in_specs=in_specs,
        out_specs=out_specs,
        check_vma=False,
    )
```

```python
import functools

import jax
import jax.numpy as jnp
from jax import lax
from jax.experimental import pallas as pl
from jax.experimental.pallas import tpu as pltpu
from jax.sharding import PartitionSpec as P

TILE = 512
ITERS = 3
LANES = 128
PIECES = TILE // LANES
DEPTH = 128
BIAS = 16
SUB = 8
CHUNK = 64
AT_ONCE = 8
FOLDS = 4
NX, NZ, NY = 4, 2, 4
MESH = pl.DeviceIdType.MESH

lowest = -1e30
epsilon = 0.1
LOG2E = 1.4426950408889634
LN2 = 0.6931471805599453
SCALE = 2.0 / epsilon * LOG2E


def lse(values):
    peak = jnp.max(values, axis=0, keepdims=True)
    return peak + jnp.log2(jnp.sum(jnp.exp2(values - peak), axis=0, keepdims=True))


def halves(values):
    high = values.astype(jnp.bfloat16)
    low = (values - high.astype(jnp.float32)).astype(jnp.bfloat16)
    return high, low


def place_points(points, reduced, kept, slot, at, dim):
    high, low = halves(points)
    size = points.shape[0]
    for ref, order in ((reduced, (high, high, low)), (kept, (high, low, high))):
        for k, part in enumerate(order):
            ref[slot, pl.ds(BIAS + k * dim + at, size), :] = part


def fill(reduced, kept, slot, dim):
    top = BIAS + 3 * dim
    for ref in (reduced, kept):
        ref[slot, top:, :] = jnp.zeros((DEPTH - top, TILE), jnp.bfloat16)
    kept[slot, :BIAS, :] = jnp.ones((BIAS, TILE), jnp.bfloat16)


def place_bias(rows, reduced, slot):
    index = lax.broadcasted_iota(jnp.int32, (BIAS, LANES), 0)
    for piece in range(PIECES):
        row = rows[piece : piece + 1, :]
        first = row.astype(jnp.bfloat16).astype(jnp.float32)
        rest = row - first
        second = rest.astype(jnp.bfloat16).astype(jnp.float32)
        third = rest - second
        tile = jnp.where(
            index == 0,
            first,
            jnp.where(index == 1, second, jnp.where(index == 2, third, 0.0)),
        )
        reduced[slot, :BIAS, piece * LANES : (piece + 1) * LANES] = tile.astype(jnp.bfloat16)


def cut(line):
    return [line[:, k * LANES : (k + 1) * LANES] for k in range(PIECES)]


def kernel(
    n_row,
    n_col,
    count,
    tiles_in,
    x_in,
    xw_in,
    y_in,
    yw_in,
    start_in,
    row_out,
    col_out,
    x_own,
    xw_own,
    y_own,
    yw_own,
    start,
    col_ids,
    row_ids,
    x_all,
    xw_all,
    y_all,
    x_reduced,
    x_kept,
    y_reduced,
    y_kept,
    x_norm,
    slots,
    col_part,
    col_recv,
    col_send,
    bias_all,
    dual_send,
    row_part,
    row_recv,
    row_total,
    tiles,
    in_sem,
    x_ssem,
    x_rsem,
    w_ssem,
    w_rsem,
    y_ssem,
    y_rsem,
    c_ssem,
    c_rsem,
    b_ssem,
    b_rsem,
    g_ssem,
    g_rsem,
    r_ssem,
    r_rsem,
):
    me_row = lax.axis_index("row")
    me_col = lax.axis_index("col")
    n_slot = slots.shape[0]
    row_blocks = x_all.shape[0]
    own_blocks = x_own.shape[0]

    def bytes_of(ref, send_sem, recv_sem, axis):
        peer = along_row(1) if axis == "row" else along_col(1)
        return pltpu.make_async_remote_copy(
            src_ref=ref,
            dst_ref=ref,
            send_sem=send_sem,
            recv_sem=recv_sem,
            device_id={axis: peer},
            device_id_type=MESH,
        )

    def along_row(d):
        return lax.rem(me_row + d, n_row)

    def along_col(d):
        return lax.rem(me_col + d, n_col)

    at_x = lax.rem(me_row, NX)
    at_z = lax.rem(lax.div(me_row, NX), NZ)
    at_y = lax.div(me_row, NX * NZ)

    def shifted(axis, shift, other, z):
        steps = (shift, other) if axis == 0 else (other, shift)
        return (
            lax.rem(at_y + steps[1], NY) * (NX * NZ)
            + lax.rem(at_z + z, NZ) * NX
            + lax.rem(at_x + steps[0], NX)
        )

    def ring(axis, step):
        return shifted(axis, step, 0, 0)

    barrier = pltpu.get_barrier_semaphore()
    fetches = [
        pltpu.make_async_copy(tiles_in, tiles, in_sem.at[4 + own_blocks]),
        pltpu.make_async_copy(y_in, y_own, in_sem.at[0]),
        pltpu.make_async_copy(xw_in, xw_own, in_sem.at[1]),
        pltpu.make_async_copy(yw_in, yw_own, in_sem.at[2]),
        pltpu.make_async_copy(start_in, start, in_sem.at[3]),
    ] + [
        pltpu.make_async_copy(x_in.at[:, pl.ds(k * TILE, TILE)], x_own.at[k], in_sem.at[4 + k])
        for k in range(own_blocks)
    ]
    for fetch in fetches:
        fetch.start()

    def greet(d, carry):
        pl.semaphore_signal(
            barrier, inc=1, device_id={"row": along_row(d)}, device_id_type=MESH
        )
        return carry

    for peer in (ring(0, 1), ring(0, 3), ring(1, 1), ring(1, 3), shifted(0, 0, 0, 1)):
        pl.semaphore_signal(barrier, inc=1, device_id={"row": peer}, device_id_type=MESH)
    for d in range(1, n_col):
        pl.semaphore_signal(
            barrier, inc=1, device_id={"col": along_col(d)}, device_id_type=MESH
        )

    def fill_y(c, carry):
        fill(y_reduced, y_kept, c, y_own.shape[0])
        return carry

    def fill_x(b, carry):
        fill(x_reduced, x_kept, b, y_own.shape[0])
        return carry

    lax.fori_loop(0, n_row, fill_y, 0)
    lax.fori_loop(0, row_blocks, fill_x, 0)
    for fetch in fetches:
        fetch.wait()
    index = lax.broadcasted_iota(jnp.int32, (n_slot, TILE), 0)

    def name_slot(k, ids):
        tile = tiles[0, 0, k]
        used = k < count[0, 0]
        row = jnp.where(used, lax.div(tile, n_row), -1)
        col = jnp.where(used, lax.rem(tile, n_row), -1)
        return (jnp.where(index == k, row, ids[0]), jnp.where(index == k, col, ids[1]))

    row_names, col_names = lax.fori_loop(0, n_slot, name_slot, (index, index))
    row_ids[...] = row_names
    col_ids[...] = col_names
    pl.semaphore_wait(barrier, 5 + n_col - 1)

    def x_copy(target, owner, turn, source):
        return pltpu.make_async_remote_copy(
            src_ref=source,
            dst_ref=x_all.at[pl.ds(owner * own_blocks, own_blocks)],
            send_sem=x_ssem.at[turn],
            recv_sem=x_rsem.at[owner],
            device_id={"col": target},
            device_id_type=MESH,
        )

    def w_copy(target, owner):
        return pltpu.make_async_remote_copy(
            src_ref=xw_own,
            dst_ref=xw_all.at[pl.ds(owner * own_blocks, own_blocks)],
            send_sem=w_ssem,
            recv_sem=w_rsem,
            device_id={"col": target},
            device_id_type=MESH,
        )

    def y_copy(target, owner, first, size, mark, source=None):
        rows = pl.ds(first * SUB, size * SUB)
        return pltpu.make_async_remote_copy(
            src_ref=y_all.at[owner, rows] if source is None else source.at[rows],
            dst_ref=y_all.at[owner, rows],
            send_sem=y_ssem,
            recv_sem=y_rsem.at[mark],
            device_id={"row": target},
            device_id_type=MESH,
        )

    def c_copy(it, target, owner):
        return pltpu.make_async_remote_copy(
            src_ref=col_part.at[it, target],
            dst_ref=col_recv.at[it, owner],
            send_sem=c_ssem.at[it],
            recv_sem=c_rsem.at[it],
            device_id={"row": target},
            device_id_type=MESH,
        )

    def b_copy(it, target, owner, mark):
        return pltpu.make_async_remote_copy(
            src_ref=col_send.at[it],
            dst_ref=bias_all.at[it, owner],
            send_sem=b_ssem.at[it],
            recv_sem=b_rsem.at[it, mark],
            device_id={"row": target},
            device_id_type=MESH,
        )

    def g_copy(target, owner):
        return pltpu.make_async_remote_copy(
            src_ref=dual_send,
            dst_ref=col_out.at[owner],
            send_sem=g_ssem,
            recv_sem=g_rsem,
            device_id={"row": target},
            device_id_type=MESH,
        )

    def r_copy(it, target, owner, at):
        return pltpu.make_async_remote_copy(
            src_ref=row_part.at[it, pl.ds(at, FOLDS)],
            dst_ref=row_recv.at[it, owner, pl.ds(at, FOLDS)],
            send_sem=r_ssem.at[it],
            recv_sem=r_rsem.at[it],
            device_id={"col": target},
            device_id_type=MESH,
        )

    dim = y_own.shape[0]
    groups = dim // SUB
    half = groups // 2
    forward, back = 1, NX - 1

    def near_first(part, turn, z):
        return 2 + (part * 2 + turn) * NZ + z

    def far_first(part):
        return 2 + 4 * NZ + part

    def near_second(part, turn, shift, z):
        return 4 + 4 * NZ + ((part * 2 + turn) * NX + shift) * NZ + z

    def far_second(part, shift):
        return 4 + 4 * NZ + 4 * NX * NZ + part * NX + shift

    def send_half(axis, part, owner, mark, source=None):
        for turn, step in enumerate((forward, back)):
            y_copy(ring(axis, step), owner, part * half, half, mark(turn), source).start()

    def relay(axis, part, owner, turn, mark, far):
        y_copy(me_row, owner, part * half, half, mark).wait_recv()
        piece = part * half + turn * (half // 2)
        step = (forward, back)[turn]
        y_copy(ring(axis, step), owner, piece, half // 2, far).start()

    def arrive(mark):
        bytes_of(y_all.at[0], y_ssem, y_rsem.at[mark], "row").wait_recv()

    def place_y(part, owner):
        at = part * half * SUB
        points = y_all[owner, at : at + half * SUB, :]
        place_points(points, y_reduced, y_kept, owner, at, dim)

    def first(part, owner, z, source=None):
        send_half(part, part, owner, lambda turn: near_first(part, turn, z), source)

    def second(part, owner, shift, z, source=None):
        mark = lambda turn: near_second(part, turn, shift, z)
        send_half(1 - part, part, owner, mark, source)

    partner = shifted(0, 0, 0, 1)
    steps = [(y, z, x) for y in range(NY) for z in range(NZ) for x in range(NX)]
    steps = sorted(steps, key=lambda s: -(min(s[0], NY - s[0]) + s[1] + min(s[2], NX - s[2])))
    peers = [(shifted(0, x, y, z), (NY - y) % NY) for y, z, x in steps[:-1]]
    far_cols = (2, 1, 3)[-(n_col - 1) :] if n_col > 1 else ()
    for part in range(2):
        y_copy(partner, me_row, part * half, half, part, y_own).start()
        first(part, me_row, 0, y_own)
    beside = me_col + 1 - 2 * lax.rem(me_col, 2)
    across = me_col + 2 - 4 * lax.rem(lax.div(me_col, 2), 2)
    if n_col > 1:
        x_copy(beside, me_col, 0, x_own).start()
    if n_col > 2:
        x_copy(across, me_col, 1, x_own).start()
    for part in range(2):
        second(part, me_row, 0, 0, y_own)
    for d in range(1, n_col):
        w_copy(along_col(d), me_col).start()

    y_norm = jnp.sum(y_own[...] * y_own[...], axis=0, keepdims=True)
    y_all[me_row] = y_own[...]
    for d in range(own_blocks):
        x_all[me_col * own_blocks + d] = x_own[d]
        xw_all[me_col * own_blocks + d] = xw_own[d]

    for part in range(2):
        y_copy(me_row, partner, part * half, half, part).wait_recv()
        first(part, partner, 1)
    for z in range(NZ):
        for part in range(2):
            for turn, step in enumerate((forward, back)):
                owner = shifted(part, NX - step, 0, z)
                relay(part, part, owner, turn, near_first(part, turn, z), far_first(part))
    for part in range(2):
        second(part, partner, 0, 1)
        for z in range(NZ):
            for shift in (forward, back):
                second(part, shifted(part, shift, 0, z), shift, z)
    for part in range(2):
        arrive(far_first(part))
        for z in range(NZ):
            second(part, shifted(part, 2, 0, z), 2, z)
    if n_col > 2:
        x_copy(me_col, across, 0, x_own).wait_recv()
        relayed = x_all.at[pl.ds(across * own_blocks, own_blocks)]
        x_copy(beside, across, 2, relayed).start()
    for part in range(2):
        for shift in range(NX):
            for z in range(NZ):
                place_y(part, shifted(part, shift, 0, z))

    for shift in (0, 1, 3, 2):
        for z in range(NZ):
            for part in range(2):
                for turn, step in enumerate((forward, back)):
                    owner = shifted(part, shift, NY - step, z)
                    near = near_second(part, turn, shift, z)
                    relay(1 - part, part, owner, turn, near, far_second(part, shift))
                    place_y(part, owner)

    if n_col > 1:
        x_copy(me_col, beside, 0, x_own).wait_recv()
    if n_col > 2:
        last = across + 1 - 2 * lax.rem(across, 2)
        x_copy(me_col, last, 0, x_own).wait_recv()
    if n_col > 1:
        others = xw_all.at[pl.ds(0, (n_col - 1) * own_blocks)]
        bytes_of(others, w_ssem, w_rsem, "col").wait_recv()

    def x_block(b, carry):
        points = x_all[b]
        place_points(points * SCALE, x_reduced, x_kept, b, 0, dim)
        norm = cut(jnp.sum(points * points, axis=0, keepdims=True))
        for k in range(PIECES):
            x_norm[b, k : k + 1, :] = norm[k]
        bias = xw_all[b] + (start[b] - x_norm[b]) * (1.0 / epsilon)
        place_bias(bias * LOG2E, x_reduced, b)
        return carry

    lax.fori_loop(0, row_blocks, x_block, 0)

    for shift in (0, 1, 3, 2):
        for part in range(2):
            arrive(far_second(part, shift))
            for z in range(NZ):
                place_y(part, shifted(part, shift, 2, z))

    def visit(reduced, kept, by_column):
        def one(slot):
            tile = tiles[0, 0, slot]
            row = lax.div(tile, n_row)
            col = lax.rem(tile, n_row)
            left, right = (row, col) if by_column else (col, row)
            score = lax.dot_general(
                reduced[left],
                kept[right],
                (((0,), (0,)), ((), ())),
                preferred_element_type=jnp.float32,
            )
            peaks, sums = [], []
            for at in range(0, TILE, CHUNK):
                part = score[at : at + CHUNK].reshape(CHUNK // SUB, SUB, TILE)
                peak = jnp.max(part, axis=0)
                peaks.append(peak)
                sums.append(jnp.sum(jnp.exp2(part - peak[None]), axis=0))
            top = functools.reduce(jnp.maximum, peaks)
            total = sum(a * jnp.exp2(b - top) for a, b in zip(sums, peaks))
            highest = jnp.max(top, axis=0, keepdims=True)
            total = jnp.sum(total * jnp.exp2(top - highest), axis=0, keepdims=True)
            slots[pl.ds(slot, 1), :] = highest + jnp.log2(total)

        def several(i, carry):
            for k in range(AT_ONCE):
                one(i * AT_ONCE + k)
            return carry

        lax.fori_loop(0, n_slot // AT_ONCE, several, 0)

    def fold(ids, block):
        return cut(lse(jnp.where(ids[...] == block, slots[...], lowest)))

    def iteration(it, carry):
        visit(x_reduced, y_kept, True)

        def col_fold(c):
            line = fold(col_ids, c)
            for k in range(PIECES):
                col_part[it, c, k : k + 1, :] = line[k]

        for at in range(0, n_row, FOLDS):
            group = (peers + [(me_row, None)])[at : at + FOLDS]
            for target, _ in group:
                col_fold(target)
            for target, mark in group:
                if mark is not None:
                    c_copy(it, target, me_row).start()
        col_recv[it, me_row] = col_part[it, me_row]
        others = col_recv.at[it, pl.ds(0, n_row - 1)]
        bytes_of(others, c_ssem.at[it], c_rsem.at[it], "row").wait_recv()
        total = lse(col_recv[it])[0]
        bias = yw_own[...] * LOG2E - total
        norm = cut(y_norm)
        col_send[it] = bias
        for k in range(PIECES):
            dual_send[k : k + 1, :] = norm[k] - (epsilon * LN2) * total[k : k + 1]

        for target, mark in peers:
            b_copy(it, target, me_row, mark).start()

        def g_start(d, inner):
            g_copy(along_row(d), me_row).start()
            return inner

        @pl.when(it == ITERS - 1)
        def _():
            lax.fori_loop(1, n_row, g_start, 0)
            col_out[me_row] = dual_send[...]

        place_bias(bias, y_reduced, me_row)

        for offset in (0, 1, 3, 2):
            size = NZ * NX - (offset == 0)
            group = bias_all.at[it, pl.ds(0, size)]
            bytes_of(group, b_ssem.at[it], b_rsem.at[it, offset], "row").wait_recv()
            for z in range(NZ):
                for x in range(NX):
                    if offset + z + x > 0:
                        owner = shifted(0, x, offset, z)
                        place_bias(bias_all[it, owner], y_reduced, owner)

        visit(y_reduced, x_kept, False)

        for at in range(0, row_blocks, FOLDS):
            for b in range(at, at + FOLDS):
                line = fold(row_ids, b)
                for k in range(PIECES):
                    row_part[it, b, k : k + 1, :] = line[k]
            for d in far_cols:
                r_copy(it, along_col(d), me_col, at).start()
        row_recv[it, me_col] = row_part[it]
        if n_col > 1:
            others = row_recv.at[it, pl.ds(0, n_col - 1)]
            bytes_of(others, r_ssem.at[it], r_rsem.at[it], "col").wait_recv()
        row_total[...] = lse(row_recv[it])[0]

        def row_bias(b, inner):
            place_bias(xw_all[b] * LOG2E - row_total[b], x_reduced, b)
            return inner

        lax.fori_loop(0, row_blocks, row_bias, 0)
        return carry

    lax.fori_loop(0, ITERS, iteration, 0)

    row_out[...] = x_norm[...] - (epsilon * LN2) * row_total[...]

    others = col_out.at[pl.ds(0, n_row - 1)]
    bytes_of(others, g_ssem, g_rsem, "row").wait_recv()
    bytes_of(others, g_ssem, g_rsem, "row").wait_send()
    for turn in range(min(n_col - 1, 3)):
        x_copy(beside, me_col, turn, x_own).wait_send()
    others = y_all.at[pl.ds(0, n_row - 1)]
    bytes_of(others, y_ssem, y_rsem.at[0], "row").wait_send()
    if n_col > 1:
        others = xw_all.at[pl.ds(0, (n_col - 1) * own_blocks)]
        bytes_of(others, w_ssem, w_rsem, "col").wait_send()
    for it in range(ITERS):
        others = col_recv.at[it, pl.ds(0, n_row - 1)]
        bytes_of(others, c_ssem.at[it], c_rsem.at[it], "row").wait_send()
        others = bias_all.at[it, pl.ds(0, n_row - 1)]
        bytes_of(others, b_ssem.at[it], b_rsem.at[it, 0], "row").wait_send()
        if n_col > 1:
            others = row_recv.at[it, pl.ds(0, n_col - 1)]
            bytes_of(others, r_ssem.at[it], r_rsem.at[it], "col").wait_send()


def per_device(
    n_row,
    n_col,
    samples,
    sample_logw,
    references,
    reference_logw,
    dual_start,
    kept_tiles,
    tile_counts,
):
    own_blocks = samples.shape[0] // TILE
    row_blocks = own_blocks * n_col
    dim = samples.shape[1]
    n_slot = kept_tiles.shape[2]
    f32 = jnp.float32
    bf16 = jnp.bfloat16
    dma = pltpu.SemaphoreType.DMA
    vmem = pltpu.VMEM
    row_dual, col_dual = pl.pallas_call(
        functools.partial(kernel, n_row, n_col),
        out_shape=(
            jax.ShapeDtypeStruct((row_blocks, PIECES, LANES), f32),
            jax.ShapeDtypeStruct((n_row, PIECES, LANES), f32),
        ),
        in_specs=[pl.BlockSpec(memory_space=pltpu.SMEM)]
        + [pl.BlockSpec(memory_space=pltpu.HBM)] * 6,
        out_specs=(pl.BlockSpec(memory_space=pltpu.VMEM),) * 2,
        scratch_shapes=[
            vmem((own_blocks, dim, TILE), f32),
            vmem((own_blocks, PIECES, LANES), f32),
            vmem((dim, TILE), f32),
            vmem((PIECES, LANES), f32),
            vmem((row_blocks, PIECES, LANES), f32),
            vmem((n_slot, TILE), jnp.int32),
            vmem((n_slot, TILE), jnp.int32),
            vmem((row_blocks, dim, TILE), f32),
            vmem((row_blocks, PIECES, LANES), f32),
            vmem((n_row, dim, TILE), f32),
            vmem((row_blocks, DEPTH, TILE), bf16),
            vmem((row_blocks, DEPTH, TILE), bf16),
            vmem((n_row, DEPTH, TILE), bf16),
            vmem((n_row, DEPTH, TILE), bf16),
            vmem((row_blocks, PIECES, LANES), f32),
            vmem((n_slot, TILE), f32),
            vmem((ITERS, n_row, PIECES, LANES), f32),
            vmem((ITERS, n_row, PIECES, LANES), f32),
            vmem((ITERS, PIECES, LANES), f32),
            vmem((ITERS, n_row, PIECES, LANES), f32),
            vmem((PIECES, LANES), f32),
            vmem((ITERS, row_blocks, PIECES, LANES), f32),
            vmem((ITERS, n_col, row_blocks, PIECES, LANES), f32),
            vmem((row_blocks, PIECES, LANES), f32),
            pltpu.SMEM(kept_tiles.shape, jnp.int32),
            dma((5 + own_blocks,)),
            dma((3,)),
            dma((n_col,)),
            dma,
            dma,
            dma,
            dma((4 + 4 * NZ + 4 * NX * NZ + 2 * NX,)),
            dma((ITERS,)),
            dma((ITERS,)),
            dma((ITERS,)),
            dma((ITERS, NY)),
            dma,
            dma,
            dma((ITERS,)),
            dma((ITERS,)),
        ],
        compiler_params=pltpu.CompilerParams(
            collective_id=0,
            has_side_effects=True,
            vmem_limit_bytes=48 * 2**20,
        ),
        name="sinkhorn",
    )(
        tile_counts,
        *[
            pltpu.with_memory_space_constraint(array, pltpu.HBM)
            for array in (
                kept_tiles,
                samples.T,
                sample_logw.reshape(own_blocks, PIECES, LANES),
                references.T,
                reference_logw.reshape(PIECES, LANES),
                dual_start.reshape(row_blocks, PIECES, LANES),
            )
        ],
    )
    return row_dual.reshape(1, -1), col_dual.reshape(1, -1)


def solution(mesh):
    n_row, n_col = mesh.shape["row"], mesh.shape["col"]
    both = ("row", "col")
    in_specs = (
        P(both, None),
        P(both),
        P(both, None),
        P(both),
        P("row", None),
        P("row", "col", None),
        P("row", "col"),
    )
    out_specs = (P("row", None), P("col", None))
    return jax.shard_map(
        functools.partial(per_device, n_row, n_col),
        mesh=mesh,
        in_specs=in_specs,
        out_specs=out_specs,
        check_vma=False,
    )
```

```python
import functools

import jax
import jax.numpy as jnp
from jax import lax
from jax.experimental import pallas as pl
from jax.experimental.pallas import tpu as pltpu
from jax.sharding import PartitionSpec as P

TILE = 512
ITERS = 3
LANES = 128
PIECES = TILE // LANES
DEPTH = 128
BIAS = 16
SUB = 8
CHUNK = 64
AT_ONCE = 8
FOLDS = 4
NX, NZ, NY = 4, 2, 4
MESH = pl.DeviceIdType.MESH

lowest = -1e30
epsilon = 0.1
LOG2E = 1.4426950408889634
LN2 = 0.6931471805599453
SCALE = 2.0 / epsilon * LOG2E


def lse(values):
    peak = jnp.max(values, axis=0, keepdims=True)
    return peak + jnp.log2(jnp.sum(jnp.exp2(values - peak), axis=0, keepdims=True))


def halves(values):
    high = values.astype(jnp.bfloat16)
    low = (values - high.astype(jnp.float32)).astype(jnp.bfloat16)
    return high, low


def place_points(points, reduced, kept, slot, at, dim):
    high, low = halves(points)
    size = points.shape[0]
    for ref, order in ((reduced, (high, high, low)), (kept, (high, low, high))):
        for k, part in enumerate(order):
            ref[slot, pl.ds(BIAS + k * dim + at, size), :] = part


def fill(reduced, kept, slot, dim):
    top = BIAS + 3 * dim
    for ref in (reduced, kept):
        ref[slot, top:, :] = jnp.zeros((DEPTH - top, TILE), jnp.bfloat16)
    kept[slot, :BIAS, :] = jnp.ones((BIAS, TILE), jnp.bfloat16)


def place_bias(rows, reduced, slot):
    index = lax.broadcasted_iota(jnp.int32, (BIAS, LANES), 0)
    for piece in range(PIECES):
        row = rows[piece : piece + 1, :]
        first = row.astype(jnp.bfloat16).astype(jnp.float32)
        rest = row - first
        second = rest.astype(jnp.bfloat16).astype(jnp.float32)
        third = rest - second
        tile = jnp.where(
            index == 0,
            first,
            jnp.where(index == 1, second, jnp.where(index == 2, third, 0.0)),
        )
        reduced[slot, :BIAS, piece * LANES : (piece + 1) * LANES] = tile.astype(jnp.bfloat16)


def cut(line):
    return [line[:, k * LANES : (k + 1) * LANES] for k in range(PIECES)]


def kernel(
    n_row,
    n_col,
    count,
    tiles_in,
    x_in,
    xw_in,
    y_in,
    yw_in,
    start_in,
    row_out,
    col_out,
    x_own,
    xw_own,
    y_own,
    yw_own,
    start,
    col_ids,
    row_ids,
    x_all,
    xw_all,
    y_all,
    x_reduced,
    x_kept,
    y_reduced,
    y_kept,
    x_norm,
    slots,
    col_part,
    col_recv,
    col_send,
    bias_all,
    dual_send,
    row_part,
    row_recv,
    row_total,
    tiles,
    in_sem,
    x_ssem,
    x_rsem,
    v_ssem,
    v_rsem,
    w_ssem,
    w_rsem,
    y_ssem,
    y_rsem,
    c_ssem,
    c_rsem,
    b_ssem,
    b_rsem,
    g_ssem,
    g_rsem,
    r_ssem,
    r_rsem,
):
    me_row = lax.axis_index("row")
    me_col = lax.axis_index("col")
    n_slot = slots.shape[0]
    row_blocks = x_all.shape[0]
    own_blocks = x_own.shape[0]

    def bytes_of(ref, send_sem, recv_sem, axis):
        peer = along_row(1) if axis == "row" else along_col(1)
        return pltpu.make_async_remote_copy(
            src_ref=ref,
            dst_ref=ref,
            send_sem=send_sem,
            recv_sem=recv_sem,
            device_id={axis: peer},
            device_id_type=MESH,
        )

    def along_row(d):
        return lax.rem(me_row + d, n_row)

    def along_col(d):
        return lax.rem(me_col + d, n_col)

    at_x = lax.rem(me_row, NX)
    at_z = lax.rem(lax.div(me_row, NX), NZ)
    at_y = lax.div(me_row, NX * NZ)

    def shifted(axis, shift, other, z):
        steps = (shift, other) if axis == 0 else (other, shift)
        return (
            lax.rem(at_y + steps[1], NY) * (NX * NZ)
            + lax.rem(at_z + z, NZ) * NX
            + lax.rem(at_x + steps[0], NX)
        )

    def ring(axis, step):
        return shifted(axis, step, 0, 0)

    barrier = pltpu.get_barrier_semaphore()
    fetches = [
        pltpu.make_async_copy(tiles_in, tiles, in_sem.at[4 + own_blocks]),
        pltpu.make_async_copy(y_in, y_own, in_sem.at[0]),
        pltpu.make_async_copy(xw_in, xw_own, in_sem.at[1]),
        pltpu.make_async_copy(yw_in, yw_own.at[0], in_sem.at[2]),
        pltpu.make_async_copy(start_in, start, in_sem.at[3]),
    ] + [
        pltpu.make_async_copy(x_in.at[:, pl.ds(k * TILE, TILE)], x_own.at[k], in_sem.at[4 + k])
        for k in range(own_blocks)
    ]
    for fetch in fetches:
        fetch.start()

    def greet(d, carry):
        pl.semaphore_signal(
            barrier, inc=1, device_id={"row": along_row(d)}, device_id_type=MESH
        )
        return carry

    for peer in (ring(0, 1), ring(0, 3), ring(1, 1), ring(1, 3), shifted(0, 0, 0, 1)):
        pl.semaphore_signal(barrier, inc=1, device_id={"row": peer}, device_id_type=MESH)
    for d in range(1, n_col):
        pl.semaphore_signal(
            barrier, inc=1, device_id={"col": along_col(d)}, device_id_type=MESH
        )

    def fill_y(c, carry):
        fill(y_reduced, y_kept, c, y_own.shape[0])
        return carry

    def fill_x(b, carry):
        fill(x_reduced, x_kept, b, y_own.shape[0])
        return carry

    lax.fori_loop(0, n_row, fill_y, 0)
    lax.fori_loop(0, row_blocks, fill_x, 0)
    for fetch in fetches:
        fetch.wait()
    index = lax.broadcasted_iota(jnp.int32, (n_slot, TILE), 0)

    def name_slot(k, ids):
        tile = tiles[0, 0, k]
        used = k < count[0, 0]
        row = jnp.where(used, lax.div(tile, n_row), -1)
        col = jnp.where(used, lax.rem(tile, n_row), -1)
        return (jnp.where(index == k, row, ids[0]), jnp.where(index == k, col, ids[1]))

    row_names, col_names = lax.fori_loop(0, n_slot, name_slot, (index, index))
    row_ids[...] = row_names
    col_ids[...] = col_names
    pl.semaphore_wait(barrier, 5 + n_col - 1)

    def x_copy(target, owner, turn, source):
        return pltpu.make_async_remote_copy(
            src_ref=source,
            dst_ref=x_all.at[pl.ds(owner * own_blocks, own_blocks)],
            send_sem=x_ssem.at[turn],
            recv_sem=x_rsem.at[owner],
            device_id={"col": target},
            device_id_type=MESH,
        )

    def w_copy(target, owner):
        return pltpu.make_async_remote_copy(
            src_ref=xw_own,
            dst_ref=xw_all.at[pl.ds(owner * own_blocks, own_blocks)],
            send_sem=w_ssem,
            recv_sem=w_rsem,
            device_id={"col": target},
            device_id_type=MESH,
        )

    def y_copy(target, owner, first, size, mark, source=None):
        rows = pl.ds(first * SUB, size * SUB)
        return pltpu.make_async_remote_copy(
            src_ref=y_all.at[owner, rows] if source is None else source.at[rows],
            dst_ref=y_all.at[owner, rows],
            send_sem=y_ssem,
            recv_sem=y_rsem.at[mark],
            device_id={"row": target},
            device_id_type=MESH,
        )

    def c_copy(it, target, owner):
        return pltpu.make_async_remote_copy(
            src_ref=col_part.at[it, target],
            dst_ref=col_recv.at[it, owner],
            send_sem=c_ssem.at[it],
            recv_sem=c_rsem.at[it],
            device_id={"row": target},
            device_id_type=MESH,
        )

    def b_copy(it, target, owner, mark):
        return pltpu.make_async_remote_copy(
            src_ref=col_send.at[it],
            dst_ref=bias_all.at[it, owner],
            send_sem=b_ssem.at[it],
            recv_sem=b_rsem.at[it, mark],
            device_id={"row": target},
            device_id_type=MESH,
        )

    def g_copy(target, owner):
        return pltpu.make_async_remote_copy(
            src_ref=dual_send,
            dst_ref=col_out.at[owner],
            send_sem=g_ssem,
            recv_sem=g_rsem,
            device_id={"row": target},
            device_id_type=MESH,
        )

    def r_copy(it, target, owner, at):
        return pltpu.make_async_remote_copy(
            src_ref=row_part.at[it, pl.ds(at, FOLDS)],
            dst_ref=row_recv.at[it, owner, pl.ds(at, FOLDS)],
            send_sem=r_ssem.at[it],
            recv_sem=r_rsem.at[it],
            device_id={"col": target},
            device_id_type=MESH,
        )

    dim = y_own.shape[0]
    groups = dim // SUB
    half = groups // 2
    forward, back = 1, NX - 1

    def near_first(part, turn, z):
        return 2 + (part * 2 + turn) * NZ + z

    def far_first(part):
        return 2 + 4 * NZ + part

    def near_second(part, turn, shift, z):
        return 4 + 4 * NZ + ((part * 2 + turn) * NX + shift) * NZ + z

    def far_second(part, shift):
        return 4 + 4 * NZ + 4 * NX * NZ + part * NX + shift

    def send_half(axis, part, owner, mark, source=None):
        for turn, step in enumerate((forward, back)):
            y_copy(ring(axis, step), owner, part * half, half, mark(turn), source).start()

    def relay(axis, part, owner, turn, mark, far):
        y_copy(me_row, owner, part * half, half, mark).wait_recv()
        piece = part * half + turn * (half // 2)
        step = (forward, back)[turn]
        y_copy(ring(axis, step), owner, piece, half // 2, far).start()

    def arrive(mark):
        bytes_of(y_all.at[0], y_ssem, y_rsem.at[mark], "row").wait_recv()

    def place_y(part, owner):
        at = part * half * SUB
        points = y_all[owner, at : at + half * SUB, :]
        place_points(points, y_reduced, y_kept, owner, at, dim)

    def first(part, owner, z, source=None):
        send_half(part, part, owner, lambda turn: near_first(part, turn, z), source)

    def second(part, owner, shift, z, source=None):
        mark = lambda turn: near_second(part, turn, shift, z)
        send_half(1 - part, part, owner, mark, source)

    partner = shifted(0, 0, 0, 1)
    steps = [(y, z, x) for y in range(NY) for z in range(NZ) for x in range(NX)]

    def hops(step):
        return min(step[0], NY - step[0]) + step[1] + min(step[2], NX - step[2])

    def opposite(step):
        return ((step[0] + NY // 2) % NY, (step[1] + NZ // 2) % NZ, (step[2] + NX // 2) % NX)

    def device(step):
        return shifted(0, step[2], step[0], step[1])

    here = (0, 0, 0)
    pairs = sorted(((hops(s), s) for s in steps if hops(s) > hops(opposite(s))), reverse=True)
    by_pairs = [s for _, step in pairs for s in (step, opposite(step))]
    close = [[s for s in steps if hops(s) == distance] for distance in (1, 2)]
    far_cols = (2, 1, 3)[-(n_col - 1) :] if n_col > 1 else ()
    for part in range(2):
        y_copy(partner, me_row, part * half, half, part, y_own).start()
        first(part, me_row, 0, y_own)
    beside = me_col + 1 - 2 * lax.rem(me_col, 2)
    across = me_col + 2 - 4 * lax.rem(lax.div(me_col, 2), 2)
    if n_col > 1:
        x_copy(beside, me_col, 0, x_own).start()
    if n_col > 2:
        x_copy(across, me_col, 1, x_own).start()
    for part in range(2):
        second(part, me_row, 0, 0, y_own)
    for d in range(1, n_col):
        w_copy(along_col(d), me_col).start()

    y_norm = jnp.sum(y_own[...] * y_own[...], axis=0, keepdims=True)
    y_all[me_row] = y_own[...]
    for d in range(own_blocks):
        x_all[me_col * own_blocks + d] = x_own[d]
        xw_all[me_col * own_blocks + d] = xw_own[d]

    for part in range(2):
        y_copy(me_row, partner, part * half, half, part).wait_recv()
        first(part, partner, 1)
    for z in range(NZ):
        for part in range(2):
            for turn, step in enumerate((forward, back)):
                owner = shifted(part, NX - step, 0, z)
                relay(part, part, owner, turn, near_first(part, turn, z), far_first(part))
    for part in range(2):
        second(part, partner, 0, 1)
        for z in range(NZ):
            for shift in (forward, back):
                second(part, shifted(part, shift, 0, z), shift, z)
    for part in range(2):
        arrive(far_first(part))
        for z in range(NZ):
            second(part, shifted(part, 2, 0, z), 2, z)
    if n_col > 2:
        x_copy(me_col, across, 0, x_own).wait_recv()
        relayed = x_all.at[pl.ds(across * own_blocks, own_blocks)]
        x_copy(beside, across, 2, relayed).start()
    for part in range(2):
        for shift in range(NX):
            for z in range(NZ):
                place_y(part, shifted(part, shift, 0, z))

    for shift in (0, 1, 3, 2):
        for z in range(NZ):
            for part in range(2):
                for turn, step in enumerate((forward, back)):
                    owner = shifted(part, shift, NY - step, z)
                    near = near_second(part, turn, shift, z)
                    relay(1 - part, part, owner, turn, near, far_second(part, shift))
                    place_y(part, owner)

    if n_col > 1:
        x_copy(me_col, beside, 0, x_own).wait_recv()
    if n_col > 2:
        last = across + 1 - 2 * lax.rem(across, 2)
        x_copy(me_col, last, 0, x_own).wait_recv()
    if n_col > 1:
        others = xw_all.at[pl.ds(0, (n_col - 1) * own_blocks)]
        bytes_of(others, w_ssem, w_rsem, "col").wait_recv()

    def x_block(b, carry):
        points = x_all[b]
        place_points(points * SCALE, x_reduced, x_kept, b, 0, dim)
        norm = cut(jnp.sum(points * points, axis=0, keepdims=True))
        for k in range(PIECES):
            x_norm[b, k : k + 1, :] = norm[k]
        bias = xw_all[b] + (start[b] - x_norm[b]) * (1.0 / epsilon)
        place_bias(bias * LOG2E, x_reduced, b)
        return carry

    lax.fori_loop(0, row_blocks, x_block, 0)

    for shift in (0, 1, 3, 2):
        for part in range(2):
            arrive(far_second(part, shift))
            for z in range(NZ):
                place_y(part, shifted(part, shift, 2, z))

    antipode = device(opposite(here))
    weights = pltpu.make_async_remote_copy(
        src_ref=yw_own.at[0],
        dst_ref=yw_own.at[1],
        send_sem=v_ssem,
        recv_sem=v_rsem,
        device_id={"row": antipode},
        device_id_type=MESH,
    )
    weights.start()

    def visit(reduced, kept, by_column):
        def one(slot):
            tile = tiles[0, 0, slot]
            row = lax.div(tile, n_row)
            col = lax.rem(tile, n_row)
            left, right = (row, col) if by_column else (col, row)
            score = lax.dot_general(
                reduced[left],
                kept[right],
                (((0,), (0,)), ((), ())),
                preferred_element_type=jnp.float32,
            )
            peaks, sums = [], []
            for at in range(0, TILE, CHUNK):
                part = score[at : at + CHUNK].reshape(CHUNK // SUB, SUB, TILE)
                peak = jnp.max(part, axis=0)
                peaks.append(peak)
                sums.append(jnp.sum(jnp.exp2(part - peak[None]), axis=0))
            top = functools.reduce(jnp.maximum, peaks)
            total = sum(a * jnp.exp2(b - top) for a, b in zip(sums, peaks))
            highest = jnp.max(top, axis=0, keepdims=True)
            total = jnp.sum(total * jnp.exp2(top - highest), axis=0, keepdims=True)
            slots[pl.ds(slot, 1), :] = highest + jnp.log2(total)

        def several(i, carry):
            for k in range(AT_ONCE):
                one(i * AT_ONCE + k)
            return carry

        lax.fori_loop(0, n_slot // AT_ONCE, several, 0)

    def fold(ids, block):
        return cut(lse(jnp.where(ids[...] == block, slots[...], lowest)))

    def iteration(it, carry):
        visit(x_reduced, y_kept, True)

        def col_fold(step):
            block, other = device(step), device(opposite(step))
            line = fold(col_ids, block)
            for k in range(PIECES):
                col_part[it, block, k : k + 1, :] = line[k]
                col_part[it, other, PIECES + k : PIECES + k + 1, :] = line[k]

        for at in range(0, n_row, FOLDS):
            group = by_pairs[at : at + FOLDS]
            for step in group:
                col_fold(step)
            for step in group:
                if step != here:
                    c_copy(it, device(step), me_row).start()
        col_recv[it, me_row] = col_part[it, me_row]

        @pl.when(it == 0)
        def _():
            weights.wait_recv()

        others = col_recv.at[it, pl.ds(0, n_row - 1)]
        bytes_of(others, c_ssem.at[it], c_rsem.at[it], "row").wait_recv()
        total = lse(col_recv[it])[0]
        bias = jnp.concatenate([yw_own[0], yw_own[1]], axis=0) * LOG2E - total
        norm = cut(y_norm)
        col_send[it] = bias
        for k in range(PIECES):
            dual_send[k : k + 1, :] = norm[k] - (epsilon * LN2) * total[k : k + 1]

        for mark in (1, 0):
            for step in close[mark]:
                b_copy(it, device(step), me_row, mark).start()

        def g_start(d, inner):
            g_copy(along_row(d), me_row).start()
            return inner

        @pl.when(it == ITERS - 1)
        def _():
            lax.fori_loop(1, n_row, g_start, 0)
            col_out[me_row] = dual_send[...]

        def place_both(rows, step):
            place_bias(rows[:PIECES], y_reduced, device(step))
            place_bias(rows[PIECES:], y_reduced, device(opposite(step)))

        place_both(bias, here)
        for mark in range(2):
            group = bias_all.at[it, pl.ds(0, len(close[mark]))]
            bytes_of(group, b_ssem.at[it], b_rsem.at[it, mark], "row").wait_recv()
            for step in close[mark]:
                place_both(bias_all[it, device(step)], step)

        visit(y_reduced, x_kept, False)

        for at in range(0, row_blocks, FOLDS):
            for b in range(at, at + FOLDS):
                line = fold(row_ids, b)
                for k in range(PIECES):
                    row_part[it, b, k : k + 1, :] = line[k]
            for d in far_cols:
                r_copy(it, along_col(d), me_col, at).start()
        row_recv[it, me_col] = row_part[it]
        if n_col > 1:
            others = row_recv.at[it, pl.ds(0, n_col - 1)]
            bytes_of(others, r_ssem.at[it], r_rsem.at[it], "col").wait_recv()
        row_total[...] = lse(row_recv[it])[0]

        def row_bias(b, inner):
            place_bias(xw_all[b] * LOG2E - row_total[b], x_reduced, b)
            return inner

        lax.fori_loop(0, row_blocks, row_bias, 0)
        return carry

    lax.fori_loop(0, ITERS, iteration, 0)

    row_out[...] = x_norm[...] - (epsilon * LN2) * row_total[...]

    others = col_out.at[pl.ds(0, n_row - 1)]
    bytes_of(others, g_ssem, g_rsem, "row").wait_recv()
    bytes_of(others, g_ssem, g_rsem, "row").wait_send()
    weights.wait_send()
    for turn in range(min(n_col - 1, 3)):
        x_copy(beside, me_col, turn, x_own).wait_send()
    others = y_all.at[pl.ds(0, n_row - 1)]
    bytes_of(others, y_ssem, y_rsem.at[0], "row").wait_send()
    if n_col > 1:
        others = xw_all.at[pl.ds(0, (n_col - 1) * own_blocks)]
        bytes_of(others, w_ssem, w_rsem, "col").wait_send()
    for it in range(ITERS):
        others = col_recv.at[it, pl.ds(0, n_row - 1)]
        bytes_of(others, c_ssem.at[it], c_rsem.at[it], "row").wait_send()
        others = bias_all.at[it, pl.ds(0, len(close[0]) + len(close[1]))]
        bytes_of(others, b_ssem.at[it], b_rsem.at[it, 0], "row").wait_send()
        if n_col > 1:
            others = row_recv.at[it, pl.ds(0, n_col - 1)]
            bytes_of(others, r_ssem.at[it], r_rsem.at[it], "col").wait_send()


def per_device(
    n_row,
    n_col,
    samples,
    sample_logw,
    references,
    reference_logw,
    dual_start,
    kept_tiles,
    tile_counts,
):
    own_blocks = samples.shape[0] // TILE
    row_blocks = own_blocks * n_col
    dim = samples.shape[1]
    n_slot = kept_tiles.shape[2]
    f32 = jnp.float32
    bf16 = jnp.bfloat16
    dma = pltpu.SemaphoreType.DMA
    vmem = pltpu.VMEM
    row_dual, col_dual = pl.pallas_call(
        functools.partial(kernel, n_row, n_col),
        out_shape=(
            jax.ShapeDtypeStruct((row_blocks, PIECES, LANES), f32),
            jax.ShapeDtypeStruct((n_row, PIECES, LANES), f32),
        ),
        in_specs=[pl.BlockSpec(memory_space=pltpu.SMEM)]
        + [pl.BlockSpec(memory_space=pltpu.HBM)] * 6,
        out_specs=(pl.BlockSpec(memory_space=pltpu.VMEM),) * 2,
        scratch_shapes=[
            vmem((own_blocks, dim, TILE), f32),
            vmem((own_blocks, PIECES, LANES), f32),
            vmem((dim, TILE), f32),
            vmem((2, PIECES, LANES), f32),
            vmem((row_blocks, PIECES, LANES), f32),
            vmem((n_slot, TILE), jnp.int32),
            vmem((n_slot, TILE), jnp.int32),
            vmem((row_blocks, dim, TILE), f32),
            vmem((row_blocks, PIECES, LANES), f32),
            vmem((n_row, dim, TILE), f32),
            vmem((row_blocks, DEPTH, TILE), bf16),
            vmem((row_blocks, DEPTH, TILE), bf16),
            vmem((n_row, DEPTH, TILE), bf16),
            vmem((n_row, DEPTH, TILE), bf16),
            vmem((row_blocks, PIECES, LANES), f32),
            vmem((n_slot, TILE), f32),
            vmem((ITERS, n_row, 2 * PIECES, LANES), f32),
            vmem((ITERS, n_row, 2 * PIECES, LANES), f32),
            vmem((ITERS, 2 * PIECES, LANES), f32),
            vmem((ITERS, n_row, 2 * PIECES, LANES), f32),
            vmem((PIECES, LANES), f32),
            vmem((ITERS, row_blocks, PIECES, LANES), f32),
            vmem((ITERS, n_col, row_blocks, PIECES, LANES), f32),
            vmem((row_blocks, PIECES, LANES), f32),
            pltpu.SMEM(kept_tiles.shape, jnp.int32),
            dma((5 + own_blocks,)),
            dma((3,)),
            dma((n_col,)),
            dma,
            dma,
            dma,
            dma,
            dma,
            dma((4 + 4 * NZ + 4 * NX * NZ + 2 * NX,)),
            dma((ITERS,)),
            dma((ITERS,)),
            dma((ITERS,)),
            dma((ITERS, 2)),
            dma,
            dma,
            dma((ITERS,)),
            dma((ITERS,)),
        ],
        compiler_params=pltpu.CompilerParams(
            collective_id=0,
            has_side_effects=True,
            vmem_limit_bytes=48 * 2**20,
        ),
        name="sinkhorn",
    )(
        tile_counts,
        *[
            pltpu.with_memory_space_constraint(array, pltpu.HBM)
            for array in (
                kept_tiles,
                samples.T,
                sample_logw.reshape(own_blocks, PIECES, LANES),
                references.T,
                reference_logw.reshape(PIECES, LANES),
                dual_start.reshape(row_blocks, PIECES, LANES),
            )
        ],
    )
    return row_dual.reshape(1, -1), col_dual.reshape(1, -1)


def solution(mesh):
    n_row, n_col = mesh.shape["row"], mesh.shape["col"]
    both = ("row", "col")
    in_specs = (
        P(both, None),
        P(both),
        P(both, None),
        P(both),
        P("row", None),
        P("row", "col", None),
        P("row", "col"),
    )
    out_specs = (P("row", None), P("col", None))
    return jax.shard_map(
        functools.partial(per_device, n_row, n_col),
        mesh=mesh,
        in_specs=in_specs,
        out_specs=out_specs,
        check_vma=False,
    )
```

```python
import functools

import jax
import jax.numpy as jnp
from jax import lax
from jax.experimental import pallas as pl
from jax.experimental.pallas import tpu as pltpu
from jax.sharding import PartitionSpec as P

TILE = 512
ITERS = 3
LANES = 128
PIECES = TILE // LANES
DEPTH = 128
BIAS = 16
SUB = 8
CHUNK = 64
AT_ONCE = 16
FOLDS = 4
NX, NZ, NY = 4, 2, 4
MESH = pl.DeviceIdType.MESH

lowest = -1e30
epsilon = 0.1
LOG2E = 1.4426950408889634
LN2 = 0.6931471805599453
SCALE = 2.0 / epsilon * LOG2E


def lse(values):
    peak = jnp.max(values, axis=0, keepdims=True)
    return peak + jnp.log2(jnp.sum(jnp.exp2(values - peak), axis=0, keepdims=True))


def halves(values):
    high = values.astype(jnp.bfloat16)
    low = (values - high.astype(jnp.float32)).astype(jnp.bfloat16)
    return high, low


def place_points(points, reduced, kept, slot, at, dim):
    high, low = halves(points)
    size = points.shape[0]
    for ref, order in ((reduced, (high, high, low)), (kept, (high, low, high))):
        for k, part in enumerate(order):
            ref[slot, pl.ds(BIAS + k * dim + at, size), :] = part


def fill(reduced, kept, slot, dim):
    top = BIAS + 3 * dim
    for ref in (reduced, kept):
        ref[slot, top:, :] = jnp.zeros((DEPTH - top, TILE), jnp.bfloat16)
    kept[slot, :BIAS, :] = jnp.ones((BIAS, TILE), jnp.bfloat16)


def place_bias(rows, reduced, slot):
    index = lax.broadcasted_iota(jnp.int32, (BIAS, LANES), 0)
    first = rows.astype(jnp.bfloat16).astype(jnp.float32)
    rest = rows - first
    second = rest.astype(jnp.bfloat16).astype(jnp.float32)
    third = rest - second
    for piece in range(PIECES):
        at = slice(piece, piece + 1)
        tile = jnp.where(
            index == 0,
            first[at],
            jnp.where(index == 1, second[at], jnp.where(index == 2, third[at], 0.0)),
        )
        reduced[slot, :BIAS, piece * LANES : (piece + 1) * LANES] = tile.astype(jnp.bfloat16)


def cut(line):
    return [line[:, k * LANES : (k + 1) * LANES] for k in range(PIECES)]


def kernel(
    n_row,
    n_col,
    count,
    tiles_in,
    x_in,
    xw_in,
    y_in,
    yw_in,
    start_in,
    row_out,
    col_out,
    x_own,
    xw_own,
    y_own,
    yw_own,
    start,
    col_ids,
    row_ids,
    x_all,
    xw_all,
    y_all,
    x_reduced,
    x_kept,
    y_reduced,
    y_kept,
    x_norm,
    slots,
    col_part,
    col_recv,
    col_send,
    bias_all,
    dual_send,
    row_part,
    row_recv,
    row_total,
    tiles,
    in_sem,
    x_ssem,
    x_rsem,
    v_ssem,
    v_rsem,
    w_ssem,
    w_rsem,
    y_ssem,
    y_rsem,
    c_ssem,
    c_rsem,
    b_ssem,
    b_rsem,
    g_ssem,
    g_rsem,
    r_ssem,
    r_rsem,
):
    me_row = lax.axis_index("row")
    me_col = lax.axis_index("col")
    n_slot = slots.shape[0]
    row_blocks = x_all.shape[0]
    own_blocks = x_own.shape[0]

    def bytes_of(ref, send_sem, recv_sem, axis):
        peer = along_row(1) if axis == "row" else along_col(1)
        return pltpu.make_async_remote_copy(
            src_ref=ref,
            dst_ref=ref,
            send_sem=send_sem,
            recv_sem=recv_sem,
            device_id={axis: peer},
            device_id_type=MESH,
        )

    def along_row(d):
        return lax.rem(me_row + d, n_row)

    def along_col(d):
        return lax.rem(me_col + d, n_col)

    at_x = lax.rem(me_row, NX)
    at_z = lax.rem(lax.div(me_row, NX), NZ)
    at_y = lax.div(me_row, NX * NZ)

    def shifted(axis, shift, other, z):
        steps = (shift, other) if axis == 0 else (other, shift)
        return (
            lax.rem(at_y + steps[1], NY) * (NX * NZ)
            + lax.rem(at_z + z, NZ) * NX
            + lax.rem(at_x + steps[0], NX)
        )

    def ring(axis, step):
        return shifted(axis, step, 0, 0)

    barrier = pltpu.get_barrier_semaphore()
    fetches = [
        pltpu.make_async_copy(tiles_in, tiles, in_sem.at[4 + own_blocks]),
        pltpu.make_async_copy(y_in, y_own, in_sem.at[0]),
        pltpu.make_async_copy(xw_in, xw_own, in_sem.at[1]),
        pltpu.make_async_copy(yw_in, yw_own.at[0], in_sem.at[2]),
        pltpu.make_async_copy(start_in, start, in_sem.at[3]),
    ] + [
        pltpu.make_async_copy(x_in.at[:, pl.ds(k * TILE, TILE)], x_own.at[k], in_sem.at[4 + k])
        for k in range(own_blocks)
    ]
    for fetch in fetches:
        fetch.start()

    def greet(d, carry):
        pl.semaphore_signal(
            barrier, inc=1, device_id={"row": along_row(d)}, device_id_type=MESH
        )
        return carry

    for peer in (ring(0, 1), ring(0, 3), ring(1, 1), ring(1, 3), shifted(0, 0, 0, 1)):
        pl.semaphore_signal(barrier, inc=1, device_id={"row": peer}, device_id_type=MESH)
    for d in range(1, n_col):
        pl.semaphore_signal(
            barrier, inc=1, device_id={"col": along_col(d)}, device_id_type=MESH
        )

    pl.semaphore_wait(barrier, 5 + n_col - 1)
    for fetch in fetches:
        fetch.wait()

    def x_copy(target, owner, turn, source):
        return pltpu.make_async_remote_copy(
            src_ref=source,
            dst_ref=x_all.at[pl.ds(owner * own_blocks, own_blocks)],
            send_sem=x_ssem.at[turn],
            recv_sem=x_rsem.at[owner],
            device_id={"col": target},
            device_id_type=MESH,
        )

    def w_copy(target, owner):
        return pltpu.make_async_remote_copy(
            src_ref=xw_own,
            dst_ref=xw_all.at[pl.ds(owner * own_blocks, own_blocks)],
            send_sem=w_ssem,
            recv_sem=w_rsem,
            device_id={"col": target},
            device_id_type=MESH,
        )

    def y_copy(target, owner, first, size, mark, source=None):
        rows = pl.ds(first * SUB, size * SUB)
        return pltpu.make_async_remote_copy(
            src_ref=y_all.at[owner, rows] if source is None else source.at[rows],
            dst_ref=y_all.at[owner, rows],
            send_sem=y_ssem,
            recv_sem=y_rsem.at[mark],
            device_id={"row": target},
            device_id_type=MESH,
        )

    def c_copy(it, target, owner):
        return pltpu.make_async_remote_copy(
            src_ref=col_part.at[it, target],
            dst_ref=col_recv.at[it, owner],
            send_sem=c_ssem.at[it],
            recv_sem=c_rsem.at[it],
            device_id={"row": target},
            device_id_type=MESH,
        )

    def b_copy(it, target, owner, mark):
        return pltpu.make_async_remote_copy(
            src_ref=col_send.at[it],
            dst_ref=bias_all.at[it, owner],
            send_sem=b_ssem.at[it],
            recv_sem=b_rsem.at[it, mark],
            device_id={"row": target},
            device_id_type=MESH,
        )

    def g_copy(target, owner):
        return pltpu.make_async_remote_copy(
            src_ref=dual_send,
            dst_ref=col_out.at[owner],
            send_sem=g_ssem,
            recv_sem=g_rsem,
            device_id={"row": target},
            device_id_type=MESH,
        )

    def r_copy(it, target, owner, at):
        return pltpu.make_async_remote_copy(
            src_ref=row_part.at[it, pl.ds(at, FOLDS)],
            dst_ref=row_recv.at[it, owner, pl.ds(at, FOLDS)],
            send_sem=r_ssem.at[it],
            recv_sem=r_rsem.at[it],
            device_id={"col": target},
            device_id_type=MESH,
        )

    dim = y_own.shape[0]
    groups = dim // SUB
    half = groups // 2
    forward, back = 1, NX - 1

    def near_first(part, turn, z):
        return 2 + (part * 2 + turn) * NZ + z

    def far_first(part):
        return 2 + 4 * NZ + part

    def near_second(part, turn, shift, z):
        return 4 + 4 * NZ + ((part * 2 + turn) * NX + shift) * NZ + z

    def far_second(part, shift):
        return 4 + 4 * NZ + 4 * NX * NZ + part * NX + shift

    def send_half(axis, part, owner, mark, source=None):
        for turn, step in enumerate((forward, back)):
            y_copy(ring(axis, step), owner, part * half, half, mark(turn), source).start()

    def relay(axis, part, owner, turn, mark, far):
        y_copy(me_row, owner, part * half, half, mark).wait_recv()
        piece = part * half + turn * (half // 2)
        step = (forward, back)[turn]
        y_copy(ring(axis, step), owner, piece, half // 2, far).start()

    def arrive(mark):
        bytes_of(y_all.at[0], y_ssem, y_rsem.at[mark], "row").wait_recv()

    def place_y(part, owner):
        at = part * half * SUB
        points = y_all[owner, at : at + half * SUB, :]
        place_points(points, y_reduced, y_kept, owner, at, dim)

    def first(part, owner, z, source=None):
        send_half(part, part, owner, lambda turn: near_first(part, turn, z), source)

    def second(part, owner, shift, z, source=None):
        mark = lambda turn: near_second(part, turn, shift, z)
        send_half(1 - part, part, owner, mark, source)

    partner = shifted(0, 0, 0, 1)
    steps = [(y, z, x) for y in range(NY) for z in range(NZ) for x in range(NX)]

    def hops(step):
        return min(step[0], NY - step[0]) + step[1] + min(step[2], NX - step[2])

    def opposite(step):
        return ((step[0] + NY // 2) % NY, (step[1] + NZ // 2) % NZ, (step[2] + NX // 2) % NX)

    def device(step):
        return shifted(0, step[2], step[0], step[1])

    here = (0, 0, 0)
    pairs = sorted(((hops(s), s) for s in steps if hops(s) > hops(opposite(s))), reverse=True)
    by_pairs = [s for _, step in pairs for s in (step, opposite(step))]
    close = [[s for s in steps if hops(s) == distance] for distance in (1, 2)]
    far_cols = (2, 1, 3)[-(n_col - 1) :] if n_col > 1 else ()
    for part in range(2):
        y_copy(partner, me_row, part * half, half, part, y_own).start()
        first(part, me_row, 0, y_own)
    beside = me_col + 1 - 2 * lax.rem(me_col, 2)
    across = me_col + 2 - 4 * lax.rem(lax.div(me_col, 2), 2)
    if n_col > 1:
        x_copy(beside, me_col, 0, x_own).start()
    if n_col > 2:
        x_copy(across, me_col, 1, x_own).start()
    for part in range(2):
        second(part, me_row, 0, 0, y_own)
    for d in range(1, n_col):
        w_copy(along_col(d), me_col).start()

    def fill_y(c, carry):
        fill(y_reduced, y_kept, c, y_own.shape[0])
        return carry

    def fill_x(b, carry):
        fill(x_reduced, x_kept, b, y_own.shape[0])
        return carry

    lax.fori_loop(0, n_row, fill_y, 0)
    lax.fori_loop(0, row_blocks, fill_x, 0)
    index = lax.broadcasted_iota(jnp.int32, (n_slot, TILE), 0)

    def name_slot(k, ids):
        tile = tiles[0, 0, k]
        used = k < count[0, 0]
        row = jnp.where(used, lax.div(tile, n_row), -1)
        col = jnp.where(used, lax.rem(tile, n_row), -1)
        return (jnp.where(index == k, row, ids[0]), jnp.where(index == k, col, ids[1]))

    row_names, col_names = lax.fori_loop(0, n_slot, name_slot, (index, index))
    row_ids[...] = row_names
    col_ids[...] = col_names
    y_norm = jnp.sum(y_own[...] * y_own[...], axis=0, keepdims=True)
    y_all[me_row] = y_own[...]
    for d in range(own_blocks):
        x_all[me_col * own_blocks + d] = x_own[d]
        xw_all[me_col * own_blocks + d] = xw_own[d]

    for part in range(2):
        y_copy(me_row, partner, part * half, half, part).wait_recv()
        first(part, partner, 1)
    for z in range(NZ):
        for part in range(2):
            for turn, step in enumerate((forward, back)):
                owner = shifted(part, NX - step, 0, z)
                relay(part, part, owner, turn, near_first(part, turn, z), far_first(part))
        for part in range(2):
            if z > 0:
                second(part, partner, 0, z)
            for shift in (forward, back):
                second(part, shifted(part, shift, 0, z), shift, z)
    for part in range(2):
        arrive(far_first(part))
        for z in range(NZ):
            second(part, shifted(part, 2, 0, z), 2, z)
    if n_col > 2:
        x_copy(me_col, across, 0, x_own).wait_recv()
        relayed = x_all.at[pl.ds(across * own_blocks, own_blocks)]
        x_copy(beside, across, 2, relayed).start()
    for part in range(2):
        for shift in range(NX):
            for z in range(NZ):
                place_y(part, shifted(part, shift, 0, z))

    for shift in (0, 1, 3, 2):
        for z in range(NZ):
            for part in range(2):
                for turn, step in enumerate((forward, back)):
                    owner = shifted(part, shift, NY - step, z)
                    near = near_second(part, turn, shift, z)
                    relay(1 - part, part, owner, turn, near, far_second(part, shift))
                    place_y(part, owner)

    if n_col > 1:
        x_copy(me_col, beside, 0, x_own).wait_recv()
    if n_col > 2:
        last = across + 1 - 2 * lax.rem(across, 2)
        x_copy(me_col, last, 0, x_own).wait_recv()
    if n_col > 1:
        others = xw_all.at[pl.ds(0, (n_col - 1) * own_blocks)]
        bytes_of(others, w_ssem, w_rsem, "col").wait_recv()

    def x_block(b, carry):
        points = x_all[b]
        place_points(points * SCALE, x_reduced, x_kept, b, 0, dim)
        norm = cut(jnp.sum(points * points, axis=0, keepdims=True))
        for k in range(PIECES):
            x_norm[b, k : k + 1, :] = norm[k]
        bias = xw_all[b] + (start[b] - x_norm[b]) * (1.0 / epsilon)
        place_bias(bias * LOG2E, x_reduced, b)
        return carry

    lax.fori_loop(0, row_blocks, x_block, 0)

    for shift in (0, 1, 3, 2):
        for part in range(2):
            arrive(far_second(part, shift))
            for z in range(NZ):
                place_y(part, shifted(part, shift, 2, z))

    antipode = device(opposite(here))
    weights = pltpu.make_async_remote_copy(
        src_ref=yw_own.at[0],
        dst_ref=yw_own.at[1],
        send_sem=v_ssem,
        recv_sem=v_rsem,
        device_id={"row": antipode},
        device_id_type=MESH,
    )
    weights.start()

    def visit(reduced, kept, by_column):
        def one(slot):
            tile = tiles[0, 0, slot]
            row = lax.div(tile, n_row)
            col = lax.rem(tile, n_row)
            left, right = (row, col) if by_column else (col, row)
            score = lax.dot_general(
                reduced[left],
                kept[right],
                (((0,), (0,)), ((), ())),
                preferred_element_type=jnp.float32,
            )
            top = total = None
            for at in range(0, TILE, CHUNK):
                part = score[at : at + CHUNK].reshape(CHUNK // SUB, SUB, TILE)
                peak = jnp.max(part, axis=0)
                before, top = top, peak if top is None else jnp.maximum(top, peak)
                fresh = jnp.sum(jnp.exp2(part - top[None]), axis=0)
                total = fresh if total is None else total * jnp.exp2(before - top) + fresh
            highest = jnp.max(top, axis=0, keepdims=True)
            total = jnp.sum(total * jnp.exp2(top - highest), axis=0, keepdims=True)
            slots[pl.ds(slot, 1), :] = highest + jnp.log2(total)

        def several(i, carry):
            for k in range(AT_ONCE):
                one(i * AT_ONCE + k)
            return carry

        lax.fori_loop(0, n_slot // AT_ONCE, several, 0)

    def fold(ids, block):
        return cut(lse(jnp.where(ids[...] == block, slots[...], lowest)))

    def iteration(it, carry):
        visit(x_reduced, y_kept, True)

        def col_fold(step):
            block, other = device(step), device(opposite(step))
            line = fold(col_ids, block)
            for k in range(PIECES):
                col_part[it, block, k : k + 1, :] = line[k]
                col_part[it, other, PIECES + k : PIECES + k + 1, :] = line[k]

        for at in range(0, n_row, FOLDS):
            group = by_pairs[at : at + FOLDS]
            for step in group:
                col_fold(step)
            for step in group:
                if step != here:
                    c_copy(it, device(step), me_row).start()
        col_recv[it, me_row] = col_part[it, me_row]

        @pl.when(it == 0)
        def _():
            weights.wait_recv()

        others = col_recv.at[it, pl.ds(0, n_row - 1)]
        bytes_of(others, c_ssem.at[it], c_rsem.at[it], "row").wait_recv()
        total = lse(col_recv[it])[0]
        bias = jnp.concatenate([yw_own[0], yw_own[1]], axis=0) * LOG2E - total
        norm = cut(y_norm)
        col_send[it] = bias
        for k in range(PIECES):
            dual_send[k : k + 1, :] = norm[k] - (epsilon * LN2) * total[k : k + 1]

        for mark in (1, 0):
            for step in close[mark]:
                b_copy(it, device(step), me_row, mark).start()

        def g_start(d, inner):
            g_copy(along_row(d), me_row).start()
            return inner

        @pl.when(it == ITERS - 1)
        def _():
            lax.fori_loop(1, n_row, g_start, 0)
            col_out[me_row] = dual_send[...]

        def place_both(rows, step):
            place_bias(rows[:PIECES], y_reduced, device(step))
            place_bias(rows[PIECES:], y_reduced, device(opposite(step)))

        place_both(bias, here)
        for mark in range(2):
            group = bias_all.at[it, pl.ds(0, len(close[mark]))]
            bytes_of(group, b_ssem.at[it], b_rsem.at[it, mark], "row").wait_recv()
            for step in close[mark]:
                place_both(bias_all[it, device(step)], step)

        visit(y_reduced, x_kept, False)

        for at in range(0, row_blocks, FOLDS):
            for b in range(at, at + FOLDS):
                line = fold(row_ids, b)
                for k in range(PIECES):
                    row_part[it, b, k : k + 1, :] = line[k]
            for d in far_cols:
                r_copy(it, along_col(d), me_col, at).start()
        row_recv[it, me_col] = row_part[it]
        if n_col > 1:
            others = row_recv.at[it, pl.ds(0, n_col - 1)]
            bytes_of(others, r_ssem.at[it], r_rsem.at[it], "col").wait_recv()
        row_total[...] = lse(row_recv[it])[0]

        def row_bias(b, inner):
            place_bias(xw_all[b] * LOG2E - row_total[b], x_reduced, b)
            return inner

        lax.fori_loop(0, row_blocks, row_bias, 0)
        return carry

    lax.fori_loop(0, ITERS, iteration, 0)

    row_out[...] = x_norm[...] - (epsilon * LN2) * row_total[...]

    others = col_out.at[pl.ds(0, n_row - 1)]
    bytes_of(others, g_ssem, g_rsem, "row").wait_recv()
    bytes_of(others, g_ssem, g_rsem, "row").wait_send()
    weights.wait_send()
    for turn in range(min(n_col - 1, 3)):
        x_copy(beside, me_col, turn, x_own).wait_send()
    others = y_all.at[pl.ds(0, n_row - 1)]
    bytes_of(others, y_ssem, y_rsem.at[0], "row").wait_send()
    if n_col > 1:
        others = xw_all.at[pl.ds(0, (n_col - 1) * own_blocks)]
        bytes_of(others, w_ssem, w_rsem, "col").wait_send()
    for it in range(ITERS):
        others = col_recv.at[it, pl.ds(0, n_row - 1)]
        bytes_of(others, c_ssem.at[it], c_rsem.at[it], "row").wait_send()
        others = bias_all.at[it, pl.ds(0, len(close[0]) + len(close[1]))]
        bytes_of(others, b_ssem.at[it], b_rsem.at[it, 0], "row").wait_send()
        if n_col > 1:
            others = row_recv.at[it, pl.ds(0, n_col - 1)]
            bytes_of(others, r_ssem.at[it], r_rsem.at[it], "col").wait_send()


def per_device(
    n_row,
    n_col,
    samples,
    sample_logw,
    references,
    reference_logw,
    dual_start,
    kept_tiles,
    tile_counts,
):
    own_blocks = samples.shape[0] // TILE
    row_blocks = own_blocks * n_col
    dim = samples.shape[1]
    n_slot = kept_tiles.shape[2]
    f32 = jnp.float32
    bf16 = jnp.bfloat16
    dma = pltpu.SemaphoreType.DMA
    vmem = pltpu.VMEM
    row_dual, col_dual = pl.pallas_call(
        functools.partial(kernel, n_row, n_col),
        out_shape=(
            jax.ShapeDtypeStruct((row_blocks, PIECES, LANES), f32),
            jax.ShapeDtypeStruct((n_row, PIECES, LANES), f32),
        ),
        in_specs=[pl.BlockSpec(memory_space=pltpu.SMEM)]
        + [pl.BlockSpec(memory_space=pltpu.HBM)] * 6,
        out_specs=(pl.BlockSpec(memory_space=pltpu.VMEM),) * 2,
        scratch_shapes=[
            vmem((own_blocks, dim, TILE), f32),
            vmem((own_blocks, PIECES, LANES), f32),
            vmem((dim, TILE), f32),
            vmem((2, PIECES, LANES), f32),
            vmem((row_blocks, PIECES, LANES), f32),
            vmem((n_slot, TILE), jnp.int32),
            vmem((n_slot, TILE), jnp.int32),
            vmem((row_blocks, dim, TILE), f32),
            vmem((row_blocks, PIECES, LANES), f32),
            vmem((n_row, dim, TILE), f32),
            vmem((row_blocks, DEPTH, TILE), bf16),
            vmem((row_blocks, DEPTH, TILE), bf16),
            vmem((n_row, DEPTH, TILE), bf16),
            vmem((n_row, DEPTH, TILE), bf16),
            vmem((row_blocks, PIECES, LANES), f32),
            vmem((n_slot, TILE), f32),
            vmem((ITERS, n_row, 2 * PIECES, LANES), f32),
            vmem((ITERS, n_row, 2 * PIECES, LANES), f32),
            vmem((ITERS, 2 * PIECES, LANES), f32),
            vmem((ITERS, n_row, 2 * PIECES, LANES), f32),
            vmem((PIECES, LANES), f32),
            vmem((ITERS, row_blocks, PIECES, LANES), f32),
            vmem((ITERS, n_col, row_blocks, PIECES, LANES), f32),
            vmem((row_blocks, PIECES, LANES), f32),
            pltpu.SMEM(kept_tiles.shape, jnp.int32),
            dma((5 + own_blocks,)),
            dma((3,)),
            dma((n_col,)),
            dma,
            dma,
            dma,
            dma,
            dma,
            dma((4 + 4 * NZ + 4 * NX * NZ + 2 * NX,)),
            dma((ITERS,)),
            dma((ITERS,)),
            dma((ITERS,)),
            dma((ITERS, 2)),
            dma,
            dma,
            dma((ITERS,)),
            dma((ITERS,)),
        ],
        compiler_params=pltpu.CompilerParams(
            collective_id=0,
            has_side_effects=True,
            vmem_limit_bytes=48 * 2**20,
        ),
        name="sinkhorn",
    )(
        tile_counts,
        *[
            pltpu.with_memory_space_constraint(array, pltpu.HBM)
            for array in (
                kept_tiles,
                samples.T,
                sample_logw.reshape(own_blocks, PIECES, LANES),
                references.T,
                reference_logw.reshape(PIECES, LANES),
                dual_start.reshape(row_blocks, PIECES, LANES),
            )
        ],
    )
    return row_dual.reshape(1, -1), col_dual.reshape(1, -1)


def solution(mesh):
    n_row, n_col = mesh.shape["row"], mesh.shape["col"]
    both = ("row", "col")
    in_specs = (
        P(both, None),
        P(both),
        P(both, None),
        P(both),
        P("row", None),
        P("row", "col", None),
        P("row", "col"),
    )
    out_specs = (P("row", None), P("col", None))
    return jax.shard_map(
        functools.partial(per_device, n_row, n_col),
        mesh=mesh,
        in_specs=in_specs,
        out_specs=out_specs,
        check_vma=False,
    )
```
